256 devices in a mesh: depth: 8 (over x, y_lo), lat: 32 (over y_hi, z, core).
Axes of the slice: x: 4, y: 4 (y_hi: 2, y_lo: 2; y = y_hi * 2 + y_lo), z: 8, core: 2. Of those that a mesh axis runs over, the one named last changes fastest.
Arguments:
- source: float32 [8, 32, 768, 64], P('depth', 'lat'), may hold values from -6 to 6
- rate: float32 [8, 32, 768], P('depth', 'lat'), may hold values from 0.002 to 2
- lat_op: float32 [8, 32, 768, 768], P('depth', 'lat'), may hold values from -1 to 1.5
- down_op: float32 [8, 32, 768, 768], P('depth', 'lat'), may hold values from -1 to 1.5
- up_op: float32 [8, 32, 768, 768], P('depth', 'lat'), may hold values from -1 to 1.5
Outputs:
- traces: float32 [8, 32, 768, 64], P('depth', 'lat')
The draws below stay inside these ranges and needn't reach their ends.
All inputs are finite; a program needn't handle non-finite values.
Results may differ from the reference program's by a relative error of at most 0.0001.
Values sent between devices are 32-bit elements; how exact they have to be, the bound alone decides.
A program may use at most 128 MiB of HBM per device.

```python
import math
import jax
import jax.numpy as jnp
from jax import lax

M = 768
R = 64
OUTER = 1
PASSES = 2
LAYERS = 8
CELLS = 32


def draw_operator(key, salt_value):
    folded = jax.random.fold_in(key, salt_value)
    full_shape = (LAYERS, CELLS, M, M)
    spread_part = jax.random.truncated_normal(folded, -4.0, 4.0, full_shape, jnp.float32)
    return 0.5 * jnp.eye(M, dtype=jnp.float32) + 0.5 / math.sqrt(M) * spread_part


def draw_lat_op(key, part):
    return draw_operator(key, 11)


def draw_down_op(key, part):
    return draw_operator(key, 23)


def draw_up_op(key, part):
    return draw_operator(key, 37)


def shard_levels(own_key, dims, cuts, smallest, top_value):
    factor_of = 1.0
    for axis_at, shards_of in cuts:
        draws = jax.random.uniform(jax.random.fold_in(jax.random.fold_in(own_key, 6), axis_at), (shards_of,), jnp.float32, smallest / len(cuts), top_value / len(cuts))
        factor_of = factor_of * jnp.repeat(jnp.exp(draws), dims[axis_at] // shards_of).reshape((-1,) + (1,) * (len(dims) - 1 - axis_at))
    return factor_of


def noise(own_key, dims, scale, limit, pieces=(), kind=jnp.bfloat16):
    factor_of = shard_levels(own_key, dims, pieces, -0.22, 0.18) if pieces else 1.0
    drawn = jax.random.normal(own_key, dims, jnp.float32) * scale * factor_of
    return jnp.minimum(jnp.maximum(drawn, -limit), limit).astype(kind)


def setup_inputs(seed: int = 0) -> dict:
    keys = jax.random.split(jax.random.key(seed), 6)
    return {
        "source": noise(keys[0], (LAYERS, CELLS, M, R), 1.0, 6.0, ((0, 8), (1, 32)), jnp.float32),
        "rate": jnp.clip(jnp.exp(math.log(2.0) - 6.9077552 * jax.random.uniform(keys[1], (LAYERS, CELLS, M), jnp.float32) ** shard_levels(keys[1], (LAYERS, CELLS, M), ((0, 8), (1, 32)), -0.2, 0.2)), 0.002, 2.0),
        "lat_op": draw_lat_op(jax.random.fold_in(keys[5], 71), 0),
        "down_op": draw_down_op(jax.random.fold_in(keys[5], 71), 0),
        "up_op": draw_up_op(jax.random.fold_in(keys[5], 71), 0),
    }


lateral_weight = 0.1
depth_weight = 0.25
relax_weight = 0.5


def propagate(matrix, vectors):
    return jnp.einsum("...ij,...jk->...ik", matrix, vectors, precision=lax.Precision.HIGHEST)


def lateral_sweep(decay, lifted, backward):
    def advance(carried, element):
        rates, values = element
        updated = rates[:, :, None] * carried + values
        return updated, updated

    start = jnp.zeros((lifted.shape[0], lifted.shape[2], lifted.shape[3]), jnp.float32)
    _, results = lax.scan(advance, start, (jnp.moveaxis(decay, 1, 0), jnp.moveaxis(lifted, 1, 0)), reverse=backward)
    return jnp.moveaxis(results, 0, 1)


def depth_sweep(operators, smoothed, backward):
    def advance(carried, element):
        matrix, values = element
        return propagate(matrix, carried) + values, carried

    start = jnp.zeros(smoothed.shape[1:], jnp.float32)
    _, results = lax.scan(advance, start, (operators, smoothed), reverse=backward)
    return results


def reference(source, rate, lat_op, down_op, up_op):
    decay = jnp.exp(-rate)
    traces = jnp.zeros_like(source)
    for outer_turn in range(OUTER):
        anchor = source + relax_weight * traces
        smoothed = anchor
        for pass_turn in range(PASSES):
            lifted = propagate(lat_op, smoothed)
            smoothed = anchor + lateral_weight * (lateral_sweep(decay, lifted, False) + lateral_sweep(decay, lifted, True))
        downward = depth_sweep(down_op, smoothed, False)
        upward = depth_sweep(up_op, smoothed, True)
        traces = smoothed + depth_weight * (downward + upward)
    return traces
```

```python
import functools

import jax
import jax.numpy as jnp
from jax import lax
from jax.experimental import pallas as pl
from jax.experimental.pallas import tpu as pltpu
from jax.sharding import PartitionSpec as P

PASSES = 2
HALVES = 2
DEPTH_CHUNKS = 4

lateral_weight = 0.1
depth_weight = 0.25

MESH = pl.DeviceIdType.MESH
F32 = jnp.float32
BF16 = jnp.bfloat16


def split(x):
    high = x.astype(BF16)
    return high, (x - high.astype(F32)).astype(BF16)


def product(x, high, low):
    rows = x.shape[0]
    x_high, x_low = split(x)
    both = jnp.dot(jnp.concatenate([x_high, x_low], axis=0), high, preferred_element_type=F32)
    return both[:rows] + (both[rows:] + jnp.dot(x_high, low, preferred_element_type=F32))


def kernel(
    layers,
    cells,
    src_hbm,
    rate_hbm,
    lat_hbm,
    down_hbm,
    up_hbm,
    out_ref,
    anchor,
    rate,
    decay,
    stage,
    lat_high,
    lat_low,
    dep_high,
    dep_low,
    fwd_src,
    fwd_rcv,
    car_src,
    car_rcv,
    bwd_src,
    bwd_rcv,
    dec_rcv,
    dec_all,
    cum,
    lefts,
    smooth,
    dep_src,
    dep_rcv,
    load_sem,
    dec_send,
    dec_recv,
    fwd_send,
    fwd_recv,
    car_send,
    car_recv,
    bwd_send,
    bwd_recv,
    dep_send,
    dep_recv,
):
    columns, order = anchor.shape
    group = cells // 2
    ring = group // 2
    width = order // 2
    half_rows = columns // HALVES
    depth_rows = columns // DEPTH_CHUNKS
    block = order // 3

    layer = lax.axis_index("depth")
    cell = lax.axis_index("lat")
    run = cell // group
    here = lax.rem(cell, group)
    z = here // 2
    core = lax.rem(here, 2)
    base = run * group

    loads = [
        pltpu.make_async_copy(src_hbm, anchor, load_sem.at[0]),
        pltpu.make_async_copy(rate_hbm, rate, load_sem.at[1]),
    ]
    for b in range(3):
        rows = pl.ds(b * block, block)
        loads.append(pltpu.make_async_copy(lat_hbm.at[rows], stage.at[0, rows], load_sem.at[2 + b]))
    loads.append(pltpu.make_async_copy(down_hbm, stage.at[1], load_sem.at[5]))
    loads.append(pltpu.make_async_copy(up_hbm, stage.at[2], load_sem.at[6]))
    for load in loads:
        load.start()

    barrier = pltpu.get_barrier_semaphore()
    for offset in range(1, group):
        pl.semaphore_signal(
            barrier, inc=1, device_id=(layer, base + lax.rem(here + offset, group)), device_id_type=MESH
        )
    other_run = (1 - run) * group + here
    pl.semaphore_signal(barrier, inc=1, device_id=(layer, other_run), device_id_type=MESH)

    @pl.when(layer > 0)
    def _():
        pl.semaphore_signal(barrier, inc=1, device_id=(layer - 1, cell), device_id_type=MESH)

    @pl.when(layer < layers - 1)
    def _():
        pl.semaphore_signal(barrier, inc=1, device_id=(layer + 1, cell), device_id_type=MESH)

    def prepare(which, b, high, low):
        rows = pl.ds(b * block, block)
        turned = stage[which, rows, :].T
        top, rest = split(turned)
        high[:, rows] = top
        low[:, rows] = rest

    loads[0].wait()
    for b in range(3):
        rows = pl.ds(b * block, block)
        loads[2 + b].wait()
        prepare(0, b, lat_high, lat_low)
        fwd_src[0, :, rows] = product(anchor[...], lat_high[:, rows], lat_low[:, rows])
    loads[1].wait()
    decay[...] = jnp.exp(-rate[...])

    edges = jnp.where(layer > 0, 1, 0) + jnp.where(layer < layers - 1, 1, 0)
    pl.semaphore_wait(barrier, group + edges)

    offsets = [ring // 2]
    for step in range(ring // 2 - 1, 0, -1):
        offsets += [step, ring - step]

    def piece(owner_z, half):
        return (
            pl.ds(pl.multiple_of(half * half_rows + 8 * (owner_z // 2), 8), 8),
            pl.ds(pl.multiple_of(lax.rem(owner_z, 2) * width, width), width),
        )

    def forward_copy(turn, half, owner_z):
        rows, modes = piece(owner_z, half)
        owner = owner_z * 2 + half
        return pltpu.make_async_remote_copy(
            src_ref=fwd_src.at[turn, rows, modes],
            dst_ref=fwd_rcv.at[turn, here],
            send_sem=fwd_send.at[turn, owner],
            recv_sem=fwd_recv.at[turn, here],
            device_id=(layer, base + owner),
            device_id_type=MESH,
        )

    def forward_own(turn):
        rows, modes = piece(z, core)
        return pltpu.make_async_copy(
            fwd_src.at[turn, rows, modes], fwd_rcv.at[turn, here], fwd_recv.at[turn, here]
        )

    def send_forward(turn, half):
        for offset in offsets:
            forward_copy(turn, half, lax.rem(z + offset, ring)).start()

        @pl.when(core != half)
        def _():
            forward_copy(turn, half, z).start()

        @pl.when(core == half)
        def _():
            forward_own(turn).start()

    def decay_copy(owner_z, half):
        owner = owner_z * 2 + half
        _, modes = piece(owner_z, half)
        return pltpu.make_async_remote_copy(
            src_ref=decay.at[:, modes],
            dst_ref=dec_rcv.at[here],
            send_sem=dec_send.at[owner],
            recv_sem=dec_recv.at[here],
            device_id=(layer, base + owner),
            device_id_type=MESH,
        )

    def decay_own():
        _, modes = piece(z, core)
        return pltpu.make_async_copy(decay.at[:, modes], dec_rcv.at[here], dec_recv.at[here])

    def all_peers(action):
        for half in range(HALVES):
            for offset in offsets:
                action(lax.rem(z + offset, ring), half)
        action(z, 1 - core)

    for half in range(HALVES):
        send_forward(0, half)
    all_peers(lambda owner_z, half: decay_copy(owner_z, half).start())
    decay_own().start()

    def carry_copy(turn):
        return pltpu.make_async_remote_copy(
            src_ref=car_src.at[turn],
            dst_ref=car_rcv.at[turn],
            send_sem=car_send.at[turn],
            recv_sem=car_recv.at[turn],
            device_id=(layer, other_run),
            device_id_type=MESH,
        )

    def backward_copy(turn, target):
        rows, modes = piece(z, core)
        return pltpu.make_async_remote_copy(
            src_ref=bwd_src.at[turn, target],
            dst_ref=bwd_rcv.at[turn, rows, modes],
            send_sem=bwd_send.at[turn, target],
            recv_sem=bwd_recv.at[turn, here],
            device_id=(layer, base + target),
            device_id_type=MESH,
        )

    def backward_own(turn):
        rows, modes = piece(z, core)
        return pltpu.make_async_copy(
            bwd_src.at[turn, here], bwd_rcv.at[turn, rows, modes], bwd_recv.at[turn, here]
        )

    def damping():
        for j in range(group):
            pltpu.make_async_copy(dec_rcv.at[j], dec_rcv.at[j], dec_recv.at[j]).wait()
        for j in range(group):
            dec_all[j] = jnp.broadcast_to(dec_rcv[j], (8, width))
        right = jnp.ones((8, width), F32)
        for j in range(group):
            right = right * dec_all[j]
            cum[j] = right
        left = jnp.ones((8, width), F32)
        for j in range(group - 1, -1, -1):
            left = left * dec_all[j]
            cum[j] = jnp.where(run == 1, cum[j], left)

    def own_sweep(turn):
        for j in range(group):
            pltpu.make_async_copy(fwd_rcv.at[turn, j], fwd_rcv.at[turn, j], fwd_recv.at[turn, j]).wait()
        right = jnp.zeros((8, width), F32)
        left = jnp.zeros((8, width), F32)
        for j in range(group):
            right = dec_all[j] * right + fwd_rcv[turn, j]
            bwd_src[turn, j] = right
            back = group - 1 - j
            left = dec_all[back] * left + fwd_rcv[turn, back]
            lefts[back] = left
        car_src[turn] = jnp.where(run == 0, right, left)
        carry_copy(turn).start()
        carry_copy(turn).wait_recv()
        carry = car_rcv[turn]
        for j in range(group):
            bwd_src[turn, j] = bwd_src[turn, j] + lefts[j] + cum[j] * carry
        for core_to in range(2):
            for offset in offsets:
                backward_copy(turn, lax.rem(z + offset, ring) * 2 + core_to).start()
        backward_copy(turn, z * 2 + 1 - core).start()
        backward_own(turn).start()

    def collected(turn, half):
        for owner_z in range(ring):
            rows, modes = piece(owner_z, half)
            ref = bwd_rcv.at[turn, rows, modes]
            pltpu.make_async_copy(ref, ref, bwd_recv.at[turn, owner_z * 2 + half]).wait()
        rows = pl.ds(half * half_rows, half_rows)
        return anchor[rows, :] + lateral_weight * bwd_rcv[turn, rows, :]

    loads[5].wait()
    for b in range(3):
        prepare(1, b, dep_high.at[0], dep_low.at[0])
    damping()
    own_sweep(0)
    loads[6].wait()
    for b in range(3):
        prepare(2, b, dep_high.at[1], dep_low.at[1])
    for half in range(HALVES):
        rows = pl.ds(half * half_rows, half_rows)
        fwd_src[1, rows, :] = product(collected(0, half), lat_high[...], lat_low[...])
        send_forward(1, half)
    own_sweep(1)

    first = jnp.where(layer >= layers // 2, 1, 0)
    second = 1 - first
    place = jnp.where(first == 0, layer, layers - 1 - layer)

    def chunk_rows(k):
        return pl.ds(pl.multiple_of(k * depth_rows, 8), depth_rows)

    def depth_copy(source, way, k):
        rows = chunk_rows(k)
        return pltpu.make_async_remote_copy(
            src_ref=source.at[rows],
            dst_ref=dep_rcv.at[way, rows],
            send_sem=dep_send.at[way, k],
            recv_sem=dep_recv.at[way, k],
            device_id=(layer + 1 - 2 * way, cell),
            device_id_type=MESH,
        )

    def arrived(way, k):
        ref = dep_rcv.at[way, chunk_rows(k)]
        pltpu.make_async_copy(ref, ref, dep_recv.at[way, k]).wait()

    for half in range(HALVES):
        rows = pl.ds(half * half_rows, half_rows)
        smooth[rows, :] = collected(1, half)

        @pl.when(place == 0)
        def _():
            for k in range(half * DEPTH_CHUNKS // HALVES, (half + 1) * DEPTH_CHUNKS // HALVES):
                depth_copy(smooth, first, k).start()

    def step(way, k):
        rows = chunk_rows(k)
        arrived(way, k)
        dep_src[way, rows, :] = smooth[rows, :] + product(
            dep_rcv[way, rows, :], dep_high[way], dep_low[way]
        )
        depth_copy(dep_src.at[way], way, k).start()

    @pl.when(place > 0)
    def _():
        @pl.loop(0, DEPTH_CHUNKS)
        def _(k):
            step(first, k)

        out_ref[...] = smooth[...] + depth_weight * dep_rcv[first]

    @pl.when(place == 0)
    def _():
        out_ref[...] = smooth[...]

        @pl.loop(0, DEPTH_CHUNKS)
        def _(k):
            arrived(second, k)

    @pl.when(place > 0)
    def _():
        @pl.loop(0, DEPTH_CHUNKS)
        def _(k):
            step(second, k)

    out_ref[...] = out_ref[...] + depth_weight * dep_rcv[second]

    for turn in range(PASSES):
        for half in range(HALVES):
            for offset in offsets:
                owner_z = lax.rem(z + offset, ring)
                forward_copy(turn, half, owner_z).wait_send()
                backward_copy(turn, owner_z * 2 + half).wait_send()
        forward_copy(turn, 1 - core, z).wait_send()
        backward_copy(turn, z * 2 + 1 - core).wait_send()
        carry_copy(turn).wait_send()
    all_peers(lambda owner_z, half: decay_copy(owner_z, half).wait_send())
    for k in range(DEPTH_CHUNKS):
        depth_copy(smooth, first, k).wait_send()

        @pl.when(place > 0)
        def _():
            depth_copy(smooth, second, k).wait_send()


def shards(source, rate, lat_op, down_op, up_op):
    order, columns = source.shape[2:]
    layers = lax.axis_size("depth")
    cells = lax.axis_size("lat")
    group = cells // 2
    width = order // 2
    any_space = pl.BlockSpec(memory_space=pl.ANY)
    vmem = pltpu.VMEM
    dma = pltpu.SemaphoreType.DMA
    traces = pl.pallas_call(
        functools.partial(kernel, layers, cells),
        name="sweeps",
        out_shape=jax.ShapeDtypeStruct((columns, order), F32),
        in_specs=[any_space] * 5,
        out_specs=pl.BlockSpec(memory_space=pltpu.VMEM),
        scratch_shapes=[
            vmem((columns, order), F32),
            vmem((1, order), F32),
            vmem((1, order), F32),
            vmem((3, order, order), F32),
            vmem((order, order), BF16),
            vmem((order, order), BF16),
            vmem((2, order, order), BF16),
            vmem((2, order, order), BF16),
            vmem((PASSES, columns, order), F32),
            vmem((PASSES, group, 8, width), F32),
            vmem((PASSES, 8, width), F32),
            vmem((PASSES, 8, width), F32),
            vmem((PASSES, group, 8, width), F32),
            vmem((PASSES, columns, order), F32),
            vmem((group, 1, width), F32),
            vmem((group, 8, width), F32),
            vmem((group, 8, width), F32),
            vmem((group, 8, width), F32),
            vmem((columns, order), F32),
            vmem((2, columns, order), F32),
            vmem((2, columns, order), F32),
            dma((7,)),
            dma((group,)),
            dma((group,)),
            dma((PASSES, group)),
            dma((PASSES, group)),
            dma((PASSES,)),
            dma((PASSES,)),
            dma((PASSES, group)),
            dma((PASSES, group)),
            dma((2, DEPTH_CHUNKS)),
            dma((2, DEPTH_CHUNKS)),
        ],
        compiler_params=pltpu.CompilerParams(
            collective_id=0, has_side_effects=True, vmem_limit_bytes=60 << 20
        ),
    )(
        source.reshape(order, columns).T,
        rate.reshape(1, order),
        lat_op.reshape(order, order),
        down_op.reshape(order, order),
        up_op.reshape(order, order),
    )
    return traces.T.reshape(1, 1, order, columns)


def solution(mesh):
    spec = P("depth", "lat", None, None)
    in_specs = (spec, P("depth", "lat", None), spec, spec, spec)
    return jax.shard_map(shards, mesh=mesh, in_specs=in_specs, out_specs=spec, check_vma=False)
```

```python
import functools

import jax
import jax.numpy as jnp
from jax import lax
from jax.experimental import pallas as pl
from jax.experimental.pallas import tpu as pltpu
from jax.sharding import PartitionSpec as P

PASSES = 2
CHUNKS = 2
DEPTH_CHUNKS = 8

lateral_weight = 0.1
depth_weight = 0.25

MESH = pl.DeviceIdType.MESH
F32 = jnp.float32
BF16 = jnp.bfloat16


def split(x):
    high = x.astype(BF16)
    return high, (x - high.astype(F32)).astype(BF16)


def product(x, high, low):
    rows = x.shape[0]
    x_high, x_low = split(x)
    both = jnp.dot(jnp.concatenate([x_high, x_low], axis=0), high, preferred_element_type=F32)
    return both[:rows] + (both[rows:] + jnp.dot(x_high, low, preferred_element_type=F32))


def kernel(
    layers,
    cells,
    src_hbm,
    rate_hbm,
    lat_hbm,
    down_hbm,
    up_hbm,
    out_ref,
    anchor,
    rate,
    decay,
    stage,
    lat_high,
    lat_low,
    dep_high,
    dep_low,
    fwd_src,
    fwd_rcv,
    car_src,
    car_rcv,
    bwd_src,
    bwd_rcv,
    dec_rcv,
    dec_all,
    cum,
    lefts,
    smooth,
    dep_src,
    dep_rcv,
    load_sem,
    dec_send,
    dec_recv,
    fwd_send,
    fwd_recv,
    car_send,
    car_recv,
    bwd_send,
    bwd_recv,
    dep_send,
    dep_recv,
):
    columns, order = anchor.shape
    group = cells // 2
    width = order // 2
    chunk = columns // CHUNKS
    owners = group // CHUNKS
    depth_rows = columns // DEPTH_CHUNKS
    per_chunk = DEPTH_CHUNKS // CHUNKS
    block = order // 3

    layer = lax.axis_index("depth")
    cell = lax.axis_index("lat")
    run = cell // group
    here = lax.rem(cell, group)
    place_in_chunk = here // CHUNKS
    own_chunk = lax.rem(here, CHUNKS)
    base = run * group

    loads = [
        pltpu.make_async_copy(src_hbm, anchor, load_sem.at[0]),
        pltpu.make_async_copy(rate_hbm, rate, load_sem.at[1]),
    ]
    for b in range(3):
        rows = pl.ds(b * block, block)
        loads.append(pltpu.make_async_copy(lat_hbm.at[rows], stage.at[0, rows], load_sem.at[2 + b]))
    loads.append(pltpu.make_async_copy(down_hbm, stage.at[1], load_sem.at[5]))
    loads.append(pltpu.make_async_copy(up_hbm, stage.at[2], load_sem.at[6]))
    for load in loads[:5]:
        load.start()

    barrier = pltpu.get_barrier_semaphore()
    for offset in range(1, group):
        pl.semaphore_signal(
            barrier, inc=1, device_id=(layer, base + lax.rem(here + offset, group)), device_id_type=MESH
        )
    other_run = (1 - run) * group + here
    pl.semaphore_signal(barrier, inc=1, device_id=(layer, other_run), device_id_type=MESH)

    @pl.when(layer > 0)
    def _():
        pl.semaphore_signal(barrier, inc=1, device_id=(layer - 1, cell), device_id_type=MESH)

    @pl.when(layer < layers - 1)
    def _():
        pl.semaphore_signal(barrier, inc=1, device_id=(layer + 1, cell), device_id_type=MESH)

    def prepare(which, b, high, low):
        rows = pl.ds(b * block, block)
        turned = stage[which, rows, :].T
        top, rest = split(turned)
        high[:, rows] = top
        low[:, rows] = rest

    loads[0].wait()
    for b in range(3):
        rows = pl.ds(b * block, block)
        loads[2 + b].wait()
        prepare(0, b, lat_high, lat_low)
        fwd_src[0, :, rows] = product(anchor[...], lat_high[:, rows], lat_low[:, rows])
    for load in loads[5:]:
        load.start()
    loads[1].wait()
    decay[...] = jnp.exp(-rate[...])

    edges = jnp.where(layer > 0, 1, 0) + jnp.where(layer < layers - 1, 1, 0)
    pl.semaphore_wait(barrier, group + edges)

    def far_first(count):
        return sorted(range(1, count), key=lambda step: -min(step, count - step))

    def piece(owner):
        part = owner // CHUNKS
        return (
            pl.ds(pl.multiple_of(lax.rem(owner, CHUNKS) * chunk + 8 * (part // 2), 8), 8),
            pl.ds(pl.multiple_of(lax.rem(part, 2) * width, width), width),
        )

    def forward_copy(turn, owner):
        return pltpu.make_async_remote_copy(
            src_ref=fwd_src.at[turn, *piece(owner)],
            dst_ref=fwd_rcv.at[turn, here],
            send_sem=fwd_send.at[turn, owner],
            recv_sem=fwd_recv.at[turn, here],
            device_id=(layer, base + owner),
            device_id_type=MESH,
        )

    def forward_own(turn):
        return pltpu.make_async_copy(
            fwd_src.at[turn, *piece(here)], fwd_rcv.at[turn, here], fwd_recv.at[turn, here]
        )

    def decay_copy(owner):
        return pltpu.make_async_remote_copy(
            src_ref=decay.at[:, piece(owner)[1]],
            dst_ref=dec_rcv.at[here],
            send_sem=dec_send.at[owner],
            recv_sem=dec_recv.at[here],
            device_id=(layer, base + owner),
            device_id_type=MESH,
        )

    def decay_own():
        return pltpu.make_async_copy(decay.at[:, piece(here)[1]], dec_rcv.at[here], dec_recv.at[here])

    def owner_of(index, offset):
        return index + CHUNKS * lax.rem(place_in_chunk + offset, owners)

    def send_forward(turn, index):
        for offset in far_first(owners):
            if turn == 0:
                decay_copy(owner_of(index, offset)).start()
            forward_copy(turn, owner_of(index, offset)).start()

        @pl.when(own_chunk != index)
        def _():
            if turn == 0:
                decay_copy(owner_of(index, 0)).start()
            forward_copy(turn, owner_of(index, 0)).start()

        @pl.when(own_chunk == index)
        def _():
            if turn == 0:
                decay_own().start()
            forward_own(turn).start()

    for index in range(CHUNKS):
        send_forward(0, index)

    def carry_copy(turn):
        return pltpu.make_async_remote_copy(
            src_ref=car_src.at[turn],
            dst_ref=car_rcv.at[turn],
            send_sem=car_send.at[turn],
            recv_sem=car_recv.at[turn],
            device_id=(layer, other_run),
            device_id_type=MESH,
        )

    def backward_copy(turn, target):
        return pltpu.make_async_remote_copy(
            src_ref=bwd_src.at[turn, target],
            dst_ref=bwd_rcv.at[turn, *piece(here)],
            send_sem=bwd_send.at[turn, target],
            recv_sem=bwd_recv.at[turn, here],
            device_id=(layer, base + target),
            device_id_type=MESH,
        )

    def backward_own(turn):
        return pltpu.make_async_copy(
            bwd_src.at[turn, here], bwd_rcv.at[turn, *piece(here)], bwd_recv.at[turn, here]
        )

    def peer(offset):
        return lax.rem(here + offset, group)

    def damping():
        for j in range(group):
            pltpu.make_async_copy(dec_rcv.at[j], dec_rcv.at[j], dec_recv.at[j]).wait()
        for j in range(group):
            dec_all[j] = jnp.broadcast_to(dec_rcv[j], (8, width))
        right = jnp.ones((8, width), F32)
        for j in range(group):
            right = right * dec_all[j]
            cum[j] = right
        left = jnp.ones((8, width), F32)
        for j in range(group - 1, -1, -1):
            left = left * dec_all[j]
            cum[j] = jnp.where(run == 1, cum[j], left)

    def own_sweep(turn, meanwhile):
        for j in range(group):
            pltpu.make_async_copy(fwd_rcv.at[turn, j], fwd_rcv.at[turn, j], fwd_recv.at[turn, j]).wait()
        right = jnp.zeros((8, width), F32)
        left = jnp.zeros((8, width), F32)
        for j in range(group):
            right = dec_all[j] * right + fwd_rcv[turn, j]
            bwd_src[turn, j] = right
            back = group - 1 - j
            left = dec_all[back] * left + fwd_rcv[turn, back]
            lefts[back] = left
        car_src[turn] = jnp.where(run == 0, right, left)
        carry_copy(turn).start()
        meanwhile()
        carry_copy(turn).wait_recv()
        carry = car_rcv[turn]
        for j in range(group):
            bwd_src[turn, j] = bwd_src[turn, j] + lefts[j] + cum[j] * carry
        for offset in far_first(group):
            backward_copy(turn, peer(offset)).start()
        backward_own(turn).start()

    def chunk_rows(index):
        return pl.ds(index * chunk, chunk)

    def collected(turn, index):
        for part in range(owners):
            owner = index + CHUNKS * part
            ref = bwd_rcv.at[turn, *piece(owner)]
            pltpu.make_async_copy(ref, ref, bwd_recv.at[turn, owner]).wait()
        rows = chunk_rows(index)
        return anchor[rows, :] + lateral_weight * bwd_rcv[turn, rows, :]

    def prepare_down():
        loads[5].wait()
        for b in range(3):
            prepare(1, b, dep_high.at[0], dep_low.at[0])

    def prepare_up():
        loads[6].wait()
        for b in range(3):
            prepare(2, b, dep_high.at[1], dep_low.at[1])

    prepare_down()
    damping()
    own_sweep(0, prepare_up)
    for index in range(CHUNKS):
        rows = chunk_rows(index)
        fwd_src[1, rows, :] = product(collected(0, index), lat_high[...], lat_low[...])
        send_forward(1, index)
    own_sweep(1, lambda: None)

    first = jnp.where(layer >= layers // 2, 1, 0)
    second = 1 - first
    place = jnp.where(first == 0, layer, layers - 1 - layer)

    def depth_chunk(k):
        return pl.ds(pl.multiple_of(k * depth_rows, 8), depth_rows)

    def depth_copy(source, way, k):
        rows = depth_chunk(k)
        return pltpu.make_async_remote_copy(
            src_ref=source.at[rows],
            dst_ref=dep_rcv.at[way, rows],
            send_sem=dep_send.at[way, k],
            recv_sem=dep_recv.at[way, k],
            device_id=(layer + 1 - 2 * way, cell),
            device_id_type=MESH,
        )

    def arrived(way, k):
        ref = dep_rcv.at[way, depth_chunk(k)]
        pltpu.make_async_copy(ref, ref, dep_recv.at[way, k]).wait()

    def step(way, k):
        rows = depth_chunk(k)
        arrived(way, k)
        dep_src[way, rows, :] = smooth[rows, :] + product(
            dep_rcv[way, rows, :], dep_high[way], dep_low[way]
        )
        depth_copy(dep_src.at[way], way, k).start()

    for index in range(CHUNKS):
        rows = chunk_rows(index)
        smooth[rows, :] = collected(1, index)

        @pl.when(place == 0)
        def _():
            for k in range(index * per_chunk, (index + 1) * per_chunk):
                depth_copy(smooth, first, k).start()
            out_ref[rows, :] = smooth[rows, :]

        @pl.when(place > 0)
        def _():
            @pl.loop(index * per_chunk, (index + 1) * per_chunk)
            def _(k):
                step(first, k)

            out_ref[rows, :] = smooth[rows, :] + depth_weight * dep_rcv[first, rows, :]

    @pl.loop(0, DEPTH_CHUNKS)
    def _(k):
        @pl.when(place == 0)
        def _():
            arrived(second, k)

        @pl.when(place > 0)
        def _():
            step(second, k)

        rows = depth_chunk(k)
        out_ref[rows, :] = out_ref[rows, :] + depth_weight * dep_rcv[second, rows, :]

    for offset in range(1, group):
        for turn in range(PASSES):
            forward_copy(turn, peer(offset)).wait_send()
            backward_copy(turn, peer(offset)).wait_send()
        decay_copy(peer(offset)).wait_send()
    for turn in range(PASSES):
        carry_copy(turn).wait_send()
    for k in range(DEPTH_CHUNKS):
        depth_copy(smooth, first, k).wait_send()

        @pl.when(place > 0)
        def _():
            depth_copy(smooth, second, k).wait_send()


def shards(source, rate, lat_op, down_op, up_op):
    order, columns = source.shape[2:]
    layers = lax.axis_size("depth")
    cells = lax.axis_size("lat")
    group = cells // 2
    width = order // 2
    any_space = pl.BlockSpec(memory_space=pl.ANY)
    vmem = pltpu.VMEM
    dma = pltpu.SemaphoreType.DMA
    traces = pl.pallas_call(
        functools.partial(kernel, layers, cells),
        name="sweeps",
        out_shape=jax.ShapeDtypeStruct((columns, order), F32),
        in_specs=[any_space] * 5,
        out_specs=pl.BlockSpec(memory_space=pltpu.VMEM),
        scratch_shapes=[
            vmem((columns, order), F32),
            vmem((1, order), F32),
            vmem((1, order), F32),
            vmem((3, order, order), F32),
            vmem((order, order), BF16),
            vmem((order, order), BF16),
            vmem((2, order, order), BF16),
            vmem((2, order, order), BF16),
            vmem((PASSES, columns, order), F32),
            vmem((PASSES, group, 8, width), F32),
            vmem((PASSES, 8, width), F32),
            vmem((PASSES, 8, width), F32),
            vmem((PASSES, group, 8, width), F32),
            vmem((PASSES, columns, order), F32),
            vmem((group, 1, width), F32),
            vmem((group, 8, width), F32),
            vmem((group, 8, width), F32),
            vmem((group, 8, width), F32),
            vmem((columns, order), F32),
            vmem((2, columns, order), F32),
            vmem((2, columns, order), F32),
            dma((7,)),
            dma((group,)),
            dma((group,)),
            dma((PASSES, group)),
            dma((PASSES, group)),
            dma((PASSES,)),
            dma((PASSES,)),
            dma((PASSES, group)),
            dma((PASSES, group)),
            dma((2, DEPTH_CHUNKS)),
            dma((2, DEPTH_CHUNKS)),
        ],
        compiler_params=pltpu.CompilerParams(
            collective_id=0, has_side_effects=True, vmem_limit_bytes=60 << 20
        ),
    )(
        source.reshape(order, columns).T,
        rate.reshape(1, order),
        lat_op.reshape(order, order),
        down_op.reshape(order, order),
        up_op.reshape(order, order),
    )
    return traces.T.reshape(1, 1, order, columns)


def solution(mesh):
    spec = P("depth", "lat", None, None)
    in_specs = (spec, P("depth", "lat", None), spec, spec, spec)
    return jax.shard_map(shards, mesh=mesh, in_specs=in_specs, out_specs=spec, check_vma=False)
```

```python
import functools

import jax
import jax.numpy as jnp
from jax import lax
from jax.experimental import pallas as pl
from jax.experimental.pallas import tpu as pltpu
from jax.sharding import PartitionSpec as P

PASSES = 2
CHUNKS = 2
DEPTH_CHUNKS = 4
PARTS = 12
RELAYED = (1, 5, 6, 10, 11)

lateral_weight = 0.1
depth_weight = 0.25

MESH = pl.DeviceIdType.MESH
F32 = jnp.float32
BF16 = jnp.bfloat16


def split(x):
    high = x.astype(BF16)
    return high, (x - high.astype(F32)).astype(BF16)


def product(x, high, low):
    rows = x.shape[0]
    x_high, x_low = split(x)
    both = jnp.dot(jnp.concatenate([x_high, x_low], axis=0), high, preferred_element_type=F32)
    return both[:rows] + (both[rows:] + jnp.dot(x_high, low, preferred_element_type=F32))


def kernel(
    layers,
    cells,
    src_hbm,
    rate_hbm,
    lat_hbm,
    down_hbm,
    up_hbm,
    out_ref,
    anchor,
    rate,
    decay,
    stage,
    lat_high,
    lat_low,
    dep_high,
    dep_low,
    fwd_src,
    fwd_rcv,
    car_src,
    car_rcv,
    bwd_src,
    bwd_rcv,
    dec_rcv,
    dec_all,
    cum,
    lefts,
    smooth,
    dep_src,
    dep_rcv,
    mate,
    relay,
    load_sem,
    dec_send,
    dec_recv,
    fwd_send,
    fwd_recv,
    car_send,
    car_recv,
    bwd_send,
    bwd_recv,
    dep_send,
    dep_recv,
    mate_send,
    mate_recv,
    part_send,
    part_recv,
    relay_recv,
):
    columns, order = anchor.shape
    group = cells // 2
    width = order // 2
    chunk = columns // CHUNKS
    owners = group // CHUNKS
    depth_rows = columns // DEPTH_CHUNKS
    per_chunk = DEPTH_CHUNKS // CHUNKS
    block = order // 3
    part_rows = order // PARTS

    layer = lax.axis_index("depth")
    cell = lax.axis_index("lat")
    run = cell // group
    here = lax.rem(cell, group)
    place_in_chunk = here // CHUNKS
    own_chunk = lax.rem(here, CHUNKS)
    base = run * group

    way = jnp.where(jnp.logical_or(layer == 3, layer >= 5), 1, 0)
    rank = jnp.where(way == 0, layer, layers - 1 - layer)
    inner = rank >= 2
    neighbour = layer + 1 - 2 * lax.rem(layer, 2)
    quad = (layer // 4) * 4
    across = jnp.where(layer < 4, layer + 2, layer - 2)
    relay_by = jnp.where(layer < 4, 3 - layer, 11 - layer)
    after = rank + jnp.where(rank < 2, 1, 2)
    chain_to = jnp.where(way == 0, after, layers - 1 - after)
    chain_slot = jnp.where(rank == 4, 1, 0)
    back_to = layer - 1 + 2 * way

    def operator_load(own, slot):
        return pltpu.make_async_copy(own, stage.at[slot], load_sem.at[4 + slot])

    def load_operators():
        for turn, (main, other) in enumerate(((down_hbm, up_hbm), (up_hbm, down_hbm))):

            @pl.when(jnp.logical_and(way == turn, rank > 0))
            def _():
                operator_load(main, 1).start()

            @pl.when(jnp.logical_and(way == turn, rank == 1))
            def _():
                operator_load(other, 2).start()

    loads = [
        pltpu.make_async_copy(src_hbm, anchor, load_sem.at[0]),
        pltpu.make_async_copy(rate_hbm, rate, load_sem.at[1]),
    ]
    for b in range(3):
        rows = pl.ds(b * block, block)
        loads.append(pltpu.make_async_copy(lat_hbm.at[rows], stage.at[0, rows], load_sem.at[2 + b]))
    for load in loads:
        load.start()

    barrier = pltpu.get_barrier_semaphore()
    for offset in range(1, group):
        pl.semaphore_signal(
            barrier, inc=1, device_id=(layer, base + lax.rem(here + offset, group)), device_id_type=MESH
        )
    other_run = (1 - run) * group + here
    pl.semaphore_signal(barrier, inc=1, device_id=(layer, other_run), device_id_type=MESH)

    for offset in range(1, 4):
        mate_layer = quad + lax.rem(layer - quad + offset, 4)
        pl.semaphore_signal(barrier, inc=1, device_id=(mate_layer, cell), device_id_type=MESH)

    @pl.when(inner)
    def _():
        pl.semaphore_signal(barrier, inc=1, device_id=(across, cell), device_id_type=MESH)

    def prepare(which, b, high, low):
        rows = pl.ds(b * block, block)
        turned = stage[which, rows, :].T
        top, rest = split(turned)
        high[:, rows] = top
        low[:, rows] = rest

    loads[0].wait()
    for b in range(3):
        rows = pl.ds(b * block, block)
        loads[2 + b].wait()
        prepare(0, b, lat_high, lat_low)
        fwd_src[0, :, rows] = product(anchor[...], lat_high[:, rows], lat_low[:, rows])
    load_operators()
    loads[1].wait()
    decay[...] = jnp.exp(-rate[...])

    pl.semaphore_wait(barrier, group + 3 + jnp.where(inner, 1, 0))

    def far_first(count):
        return sorted(range(1, count), key=lambda step: -min(step, count - step))

    def piece(owner):
        part = owner // CHUNKS
        return (
            pl.ds(pl.multiple_of(lax.rem(owner, CHUNKS) * chunk + 8 * (part // 2), 8), 8),
            pl.ds(pl.multiple_of(lax.rem(part, 2) * width, width), width),
        )

    def forward_copy(turn, owner):
        return pltpu.make_async_remote_copy(
            src_ref=fwd_src.at[turn, *piece(owner)],
            dst_ref=fwd_rcv.at[turn, here],
            send_sem=fwd_send.at[turn],
            recv_sem=fwd_recv.at[turn],
            device_id=(layer, base + owner),
            device_id_type=MESH,
        )

    def forward_own(turn):
        return pltpu.make_async_copy(
            fwd_src.at[turn, *piece(here)], fwd_rcv.at[turn, here], fwd_recv.at[turn]
        )

    def decay_copy(owner):
        return pltpu.make_async_remote_copy(
            src_ref=decay.at[:, piece(owner)[1]],
            dst_ref=dec_rcv.at[here],
            send_sem=dec_send,
            recv_sem=dec_recv,
            device_id=(layer, base + owner),
            device_id_type=MESH,
        )

    def decay_own():
        return pltpu.make_async_copy(decay.at[:, piece(here)[1]], dec_rcv.at[here], dec_recv)

    def owner_of(index, offset):
        return index + CHUNKS * lax.rem(place_in_chunk + offset, owners)

    def send_forward(turn, index):
        for offset in far_first(owners):
            if turn == 0:
                decay_copy(owner_of(index, offset)).start()
            forward_copy(turn, owner_of(index, offset)).start()

        @pl.when(own_chunk != index)
        def _():
            if turn == 0:
                decay_copy(owner_of(index, 0)).start()
            forward_copy(turn, owner_of(index, 0)).start()

        @pl.when(own_chunk == index)
        def _():
            if turn == 0:
                decay_own().start()
            forward_own(turn).start()

    for index in range(CHUNKS):
        send_forward(0, index)

    def carry_copy(turn):
        return pltpu.make_async_remote_copy(
            src_ref=car_src.at[turn],
            dst_ref=car_rcv.at[turn],
            send_sem=car_send.at[turn],
            recv_sem=car_recv.at[turn],
            device_id=(layer, other_run),
            device_id_type=MESH,
        )

    def backward_copy(turn, target):
        return pltpu.make_async_remote_copy(
            src_ref=bwd_src.at[turn, target],
            dst_ref=bwd_rcv.at[turn, *piece(here)],
            send_sem=bwd_send.at[turn],
            recv_sem=bwd_recv.at[turn, own_chunk],
            device_id=(layer, base + target),
            device_id_type=MESH,
        )

    def backward_own(turn):
        return pltpu.make_async_copy(
            bwd_src.at[turn, here], bwd_rcv.at[turn, *piece(here)], bwd_recv.at[turn, own_chunk]
        )

    def peer(offset):
        return lax.rem(here + offset, group)

    def all_of(ref, sem):
        pltpu.make_async_copy(ref, ref, sem).wait()

    def damping():
        all_of(dec_rcv, dec_recv)
        for j in range(group):
            dec_all[j] = jnp.broadcast_to(dec_rcv[j], (8, width))
        right = jnp.ones((8, width), F32)
        for j in range(group):
            right = right * dec_all[j]
            cum[j] = right
        left = jnp.ones((8, width), F32)
        for j in range(group - 1, -1, -1):
            left = left * dec_all[j]
            cum[j] = jnp.where(run == 1, cum[j], left)

    def part(b):
        return pl.ds(b * part_rows, part_rows)

    def third(b):
        return 3 * b // PARTS

    def relay_part(b):
        return relay.at[part(RELAYED.index(b))]

    def ship_copy(b, source):
        relayed = b in RELAYED
        return pltpu.make_async_remote_copy(
            src_ref=source.at[part(b)],
            dst_ref=relay_part(b) if relayed else stage.at[2, part(b)],
            send_sem=part_send,
            recv_sem=relay_recv.at[RELAYED.index(b)] if relayed else part_recv.at[third(b)],
            device_id=(relay_by if relayed else neighbour, cell),
            device_id_type=MESH,
        )

    def ship(*parts):
        for turn, other in enumerate((up_hbm, down_hbm)):

            @pl.when(jnp.logical_and(inner, way == turn))
            def _():
                for b in parts:
                    ship_copy(b, other).start()

    def hand_on(*parts):
        @pl.when(rank < 2)
        def _():
            for b in parts:
                all_of(relay_part(b), relay_recv.at[RELAYED.index(b)])
                pltpu.make_async_remote_copy(
                    src_ref=relay_part(b),
                    dst_ref=stage.at[2, part(b)],
                    send_sem=part_send,
                    recv_sem=part_recv.at[third(b)],
                    device_id=(across, cell),
                    device_id_type=MESH,
                ).start()

    def own_sweep(turn, meanwhile):
        all_of(fwd_rcv.at[turn], fwd_recv.at[turn])
        right = jnp.zeros((8, width), F32)
        left = jnp.zeros((8, width), F32)
        for j in range(group):
            right = dec_all[j] * right + fwd_rcv[turn, j]
            bwd_src[turn, j] = right
            back = group - 1 - j
            left = dec_all[back] * left + fwd_rcv[turn, back]
            lefts[back] = left
        car_src[turn] = jnp.where(run == 0, right, left)
        carry_copy(turn).start()
        meanwhile()
        carry_copy(turn).wait_recv()
        carry = car_rcv[turn]
        for j in range(group):
            bwd_src[turn, j] = bwd_src[turn, j] + lefts[j] + cum[j] * carry
        for offset in far_first(group):
            backward_copy(turn, peer(offset)).start()
        backward_own(turn).start()

    def chunk_rows(index):
        return pl.ds(index * chunk, chunk)

    def collected(turn, index):
        rows = chunk_rows(index)
        all_of(bwd_rcv.at[turn, rows], bwd_recv.at[turn, index])
        return anchor[rows, :] + lateral_weight * bwd_rcv[turn, rows, :]

    def prepare_main():
        @pl.when(rank > 0)
        def _():
            operator_load(down_hbm, 1).wait()
            for b in range(3):
                prepare(1, b, dep_high.at[0], dep_low.at[0])

    def prepare_other(b):
        all_of(stage.at[2, pl.ds(b * block, block)], part_recv.at[b])
        prepare(2, b, dep_high.at[1], dep_low.at[1])

    def first_meanwhile():
        ship(2, 3, 4)

        @pl.when(rank == 1)
        def _():
            operator_load(down_hbm, 2).wait()
            for b in range(3):
                prepare(2, b, dep_high.at[1], dep_low.at[1])

    def second_meanwhile():
        ship(7, 8, 9)
        hand_on(6)

        @pl.when(inner)
        def _():
            prepare_other(0)

    ship(1, 0)
    prepare_main()
    damping()
    own_sweep(0, first_meanwhile)
    ship(5, 6)
    hand_on(1)
    for index in range(CHUNKS):
        rows = chunk_rows(index)
        fwd_src[1, rows, :] = product(collected(0, index), lat_high[...], lat_low[...])
        send_forward(1, index)
    hand_on(5)
    own_sweep(1, second_meanwhile)
    ship(10, 11)

    @pl.when(inner)
    def _():
        prepare_other(1)

    def depth_chunk(k):
        return pl.ds(pl.multiple_of(k * depth_rows, 8), depth_rows)

    def depth_copy(source, k, send, slot, target):
        rows = depth_chunk(k)
        return pltpu.make_async_remote_copy(
            src_ref=source.at[rows],
            dst_ref=dep_rcv.at[slot, rows],
            send_sem=dep_send.at[send],
            recv_sem=dep_recv.at[slot, k],
            device_id=(target, cell),
            device_id_type=MESH,
        )

    def arrived(slot, k):
        ref = dep_rcv.at[slot, depth_chunk(k)]
        pltpu.make_async_copy(ref, ref, dep_recv.at[slot, k]).wait()

    def mate_copy(index):
        rows = chunk_rows(index)
        return pltpu.make_async_remote_copy(
            src_ref=smooth.at[rows],
            dst_ref=mate.at[rows],
            send_sem=mate_send,
            recv_sem=mate_recv,
            device_id=(neighbour, cell),
            device_id_type=MESH,
        )

    for index in range(CHUNKS):
        rows = chunk_rows(index)
        smooth[rows, :] = collected(1, index)

        @pl.when(rank == 0)
        def _():
            for k in range(index * per_chunk, (index + 1) * per_chunk):
                depth_copy(smooth, k, 0, 0, chain_to).start()

        @pl.when(inner)
        def _():
            mate_copy(index).start()

    hand_on(10, 11)

    def applied(c, which):
        return product(c, dep_high[which], dep_low[which])

    @pl.when(rank == 1)
    def _():
        @pl.loop(0, DEPTH_CHUNKS)
        def _(k):
            rows = depth_chunk(k)
            arrived(0, k)
            dep_src[0, rows, :] = smooth[rows, :] + applied(dep_rcv[0, rows, :], 0)
            depth_copy(dep_src.at[0], k, 0, 0, chain_to).start()
            out_ref[rows, :] = smooth[rows, :] + depth_weight * dep_rcv[0, rows, :]

        @pl.loop(0, DEPTH_CHUNKS)
        def _(k):
            rows = depth_chunk(k)
            arrived(1, k)
            dep_src[1, rows, :] = smooth[rows, :] + applied(dep_rcv[1, rows, :], 1)
            depth_copy(dep_src.at[1], k, 1, 1, back_to).start()
            out_ref[rows, :] = out_ref[rows, :] + depth_weight * dep_rcv[1, rows, :]

    @pl.when(rank == 0)
    def _():
        @pl.loop(0, DEPTH_CHUNKS)
        def _(k):
            rows = depth_chunk(k)
            arrived(1, k)
            out_ref[rows, :] = smooth[rows, :] + depth_weight * dep_rcv[1, rows, :]

    @pl.when(inner)
    def _():
        prepare_other(2)
        all_of(mate, mate_recv)

        @pl.loop(0, DEPTH_CHUNKS)
        def _(k):
            rows = depth_chunk(k)
            arrived(0, k)
            near = smooth[rows, :] + applied(dep_rcv[0, rows, :], 0)
            dep_src[0, rows, :] = near
            dep_src[1, rows, :] = mate[rows, :] + applied(near, 1)
            depth_copy(dep_src.at[1], k, 0, chain_slot, chain_to).start()
            depth_copy(dep_src.at[0], k, 1, 1, neighbour).start()
            out_ref[rows, :] = smooth[rows, :] + depth_weight * dep_rcv[0, rows, :]

        @pl.loop(0, DEPTH_CHUNKS)
        def _(k):
            rows = depth_chunk(k)
            arrived(1, k)
            out_ref[rows, :] = out_ref[rows, :] + depth_weight * dep_rcv[1, rows, :]

    peers = pl.ds(0, group - 1)
    for turn in range(PASSES):
        all_of(fwd_rcv.at[turn, peers], fwd_send.at[turn])
        all_of(bwd_src.at[turn, peers], bwd_send.at[turn])
        all_of(car_src.at[turn], car_send.at[turn])
    all_of(dec_rcv.at[peers], dec_send)
    all_of(smooth, dep_send.at[0])

    @pl.when(rank > 0)
    def _():
        all_of(smooth, dep_send.at[1])

    @pl.when(inner)
    def _():
        all_of(smooth, mate_send)
        all_of(stage.at[0], part_send)

    @pl.when(rank < 2)
    def _():
        all_of(relay, part_send)


def shards(source, rate, lat_op, down_op, up_op):
    order, columns = source.shape[2:]
    layers = lax.axis_size("depth")
    cells = lax.axis_size("lat")
    group = cells // 2
    width = order // 2
    any_space = pl.BlockSpec(memory_space=pl.ANY)
    vmem = pltpu.VMEM
    dma = pltpu.SemaphoreType.DMA
    traces = pl.pallas_call(
        functools.partial(kernel, layers, cells),
        name="sweeps",
        out_shape=jax.ShapeDtypeStruct((columns, order), F32),
        in_specs=[any_space] * 5,
        out_specs=pl.BlockSpec(memory_space=pltpu.VMEM),
        scratch_shapes=[
            vmem((columns, order), F32),
            vmem((1, order), F32),
            vmem((1, order), F32),
            vmem((3, order, order), F32),
            vmem((order, order), BF16),
            vmem((order, order), BF16),
            vmem((2, order, order), BF16),
            vmem((2, order, order), BF16),
            vmem((PASSES, columns, order), F32),
            vmem((PASSES, group, 8, width), F32),
            vmem((PASSES, 8, width), F32),
            vmem((PASSES, 8, width), F32),
            vmem((PASSES, group, 8, width), F32),
            vmem((PASSES, columns, order), F32),
            vmem((group, 1, width), F32),
            vmem((group, 8, width), F32),
            vmem((group, 8, width), F32),
            vmem((group, 8, width), F32),
            vmem((columns, order), F32),
            vmem((2, columns, order), F32),
            vmem((2, columns, order), F32),
            vmem((columns, order), F32),
            vmem((len(RELAYED) * (order // PARTS), order), F32),
            dma((7,)),
            dma,
            dma,
            dma((PASSES,)),
            dma((PASSES,)),
            dma((PASSES,)),
            dma((PASSES,)),
            dma((PASSES,)),
            dma((PASSES, CHUNKS)),
            dma((2,)),
            dma((2, DEPTH_CHUNKS)),
            dma,
            dma,
            dma,
            dma((3,)),
            dma((len(RELAYED),)),
        ],
        compiler_params=pltpu.CompilerParams(
            collective_id=0, has_side_effects=True, vmem_limit_bytes=60 << 20
        ),
    )(
        source.reshape(order, columns).T,
        rate.reshape(1, order),
        lat_op.reshape(order, order),
        down_op.reshape(order, order),
        up_op.reshape(order, order),
    )
    return traces.T.reshape(1, 1, order, columns)


def solution(mesh):
    spec = P("depth", "lat", None, None)
    in_specs = (spec, P("depth", "lat", None), spec, spec, spec)
    return jax.shard_map(shards, mesh=mesh, in_specs=in_specs, out_specs=spec, check_vma=False)
```

```python
import functools

import jax
import jax.numpy as jnp
from jax import lax
from jax.experimental import pallas as pl
from jax.experimental.pallas import tpu as pltpu
from jax.sharding import PartitionSpec as P

PASSES = 2
CHUNKS = 2
DEPTH_CHUNKS = 4
PARTS = 12
RELAYED = (1, 5, 6, 10, 11)

lateral_weight = 0.1
depth_weight = 0.25

MESH = pl.DeviceIdType.MESH
F32 = jnp.float32
BF16 = jnp.bfloat16


def split(x):
    high = x.astype(BF16)
    return high, (x - high.astype(F32)).astype(BF16)


def product(x, high, low):
    rows = x.shape[0]
    x_high, x_low = split(x)
    both = jnp.dot(jnp.concatenate([x_high, x_low], axis=0), high, preferred_element_type=F32)
    return both[:rows] + (both[rows:] + jnp.dot(x_high, low, preferred_element_type=F32))


def kernel(
    layers,
    cells,
    src_hbm,
    rate_hbm,
    lat_hbm,
    down_hbm,
    up_hbm,
    out_ref,
    anchor,
    rate,
    decay,
    stage,
    lat_high,
    lat_low,
    dep_high,
    dep_low,
    fwd_src,
    fwd_rcv,
    car_src,
    car_rcv,
    bwd_src,
    bwd_rcv,
    dec_rcv,
    dec_all,
    cum,
    lefts,
    smooth,
    dep_src,
    dep_rcv,
    mate,
    relay,
    load_sem,
    dec_send,
    dec_recv,
    fwd_send,
    fwd_recv,
    car_send,
    car_recv,
    bwd_send,
    bwd_recv,
    dep_send,
    dep_recv,
    mate_send,
    mate_recv,
    part_send,
    part_recv,
    relay_recv,
):
    columns, order = anchor.shape
    group = cells // 2
    width = order // 2
    chunk = columns // CHUNKS
    owners = group // CHUNKS
    depth_rows = columns // DEPTH_CHUNKS
    per_chunk = DEPTH_CHUNKS // CHUNKS
    block = order // 3
    part_rows = order // PARTS

    layer = lax.axis_index("depth")
    cell = lax.axis_index("lat")
    run = cell // group
    here = lax.rem(cell, group)
    place_in_chunk = here // CHUNKS
    own_chunk = lax.rem(here, CHUNKS)
    base = run * group

    way = jnp.where(jnp.logical_or(layer == 3, layer >= 5), 1, 0)
    rank = jnp.where(way == 0, layer, layers - 1 - layer)
    inner = rank >= 2
    neighbour = layer + 1 - 2 * lax.rem(layer, 2)
    quad = (layer // 4) * 4
    across = jnp.where(layer < 4, layer + 2, layer - 2)
    relay_by = jnp.where(layer < 4, 3 - layer, 11 - layer)
    after = rank + jnp.where(rank < 2, 1, 2)
    chain_to = jnp.where(way == 0, after, layers - 1 - after)
    chain_slot = jnp.where(rank == 4, 1, 0)
    back_to = layer - 1 + 2 * way

    def operator_load(own, slot):
        return pltpu.make_async_copy(own, stage.at[slot], load_sem.at[4 + slot])

    def load_operators():
        for turn, (main, other) in enumerate(((down_hbm, up_hbm), (up_hbm, down_hbm))):

            @pl.when(jnp.logical_and(way == turn, rank > 0))
            def _():
                operator_load(main, 1).start()

            @pl.when(jnp.logical_and(way == turn, rank == 1))
            def _():
                operator_load(other, 2).start()

    loads = [
        pltpu.make_async_copy(src_hbm, anchor, load_sem.at[0]),
        pltpu.make_async_copy(rate_hbm, rate, load_sem.at[1]),
    ]
    for b in range(3):
        rows = pl.ds(b * block, block)
        loads.append(pltpu.make_async_copy(lat_hbm.at[rows], stage.at[0, rows], load_sem.at[2 + b]))
    for load in loads:
        load.start()

    barrier = pltpu.get_barrier_semaphore()
    for offset in range(1, group):
        pl.semaphore_signal(
            barrier, inc=1, device_id=(layer, base + lax.rem(here + offset, group)), device_id_type=MESH
        )
    other_run = (1 - run) * group + here
    pl.semaphore_signal(barrier, inc=1, device_id=(layer, other_run), device_id_type=MESH)

    for offset in range(1, 4):
        mate_layer = quad + lax.rem(layer - quad + offset, 4)
        pl.semaphore_signal(barrier, inc=1, device_id=(mate_layer, cell), device_id_type=MESH)

    @pl.when(inner)
    def _():
        pl.semaphore_signal(barrier, inc=1, device_id=(across, cell), device_id_type=MESH)

    def prepare(which, b, high, low):
        rows = pl.ds(b * block, block)
        turned = stage[which, rows, :].T
        top, rest = split(turned)
        high[:, rows] = top
        low[:, rows] = rest

    loads[0].wait()
    for b in range(3):
        rows = pl.ds(b * block, block)
        loads[2 + b].wait()
        prepare(0, b, lat_high, lat_low)
        fwd_src[0, :, rows] = product(anchor[...], lat_high[:, rows], lat_low[:, rows])
    load_operators()
    loads[1].wait()
    decay[...] = jnp.exp(-rate[...])

    pl.semaphore_wait(barrier, group + 3 + jnp.where(inner, 1, 0))

    def far_first(count):
        return sorted(range(1, count), key=lambda step: -min(step, count - step))

    def piece(owner):
        part = owner // CHUNKS
        return (
            pl.ds(pl.multiple_of(lax.rem(owner, CHUNKS) * chunk + 8 * (part // 2), 8), 8),
            pl.ds(pl.multiple_of(lax.rem(part, 2) * width, width), width),
        )

    def forward_copy(turn, owner):
        return pltpu.make_async_remote_copy(
            src_ref=fwd_src.at[turn, *piece(owner)],
            dst_ref=fwd_rcv.at[turn, here],
            send_sem=fwd_send.at[turn],
            recv_sem=fwd_recv.at[turn],
            device_id=(layer, base + owner),
            device_id_type=MESH,
        )

    def forward_own(turn):
        return pltpu.make_async_copy(
            fwd_src.at[turn, *piece(here)], fwd_rcv.at[turn, here], fwd_recv.at[turn]
        )

    def decay_copy(owner):
        return pltpu.make_async_remote_copy(
            src_ref=decay.at[:, piece(owner)[1]],
            dst_ref=dec_rcv.at[here],
            send_sem=dec_send,
            recv_sem=dec_recv,
            device_id=(layer, base + owner),
            device_id_type=MESH,
        )

    def decay_own():
        return pltpu.make_async_copy(decay.at[:, piece(here)[1]], dec_rcv.at[here], dec_recv)

    def owner_of(index, offset):
        return index + CHUNKS * lax.rem(place_in_chunk + offset, owners)

    def send_forward(turn, index):
        for offset in far_first(owners):
            if turn == 0:
                decay_copy(owner_of(index, offset)).start()
            forward_copy(turn, owner_of(index, offset)).start()

        @pl.when(own_chunk != index)
        def _():
            if turn == 0:
                decay_copy(owner_of(index, 0)).start()
            forward_copy(turn, owner_of(index, 0)).start()

        @pl.when(own_chunk == index)
        def _():
            if turn == 0:
                decay_own().start()
            forward_own(turn).start()

    for index in range(CHUNKS):
        send_forward(0, index)

    def carry_copy(turn):
        return pltpu.make_async_remote_copy(
            src_ref=car_src.at[turn],
            dst_ref=car_rcv.at[turn],
            send_sem=car_send.at[turn],
            recv_sem=car_recv.at[turn],
            device_id=(layer, other_run),
            device_id_type=MESH,
        )

    def backward_copy(turn, target):
        return pltpu.make_async_remote_copy(
            src_ref=bwd_src.at[turn, target],
            dst_ref=bwd_rcv.at[turn, *piece(here)],
            send_sem=bwd_send.at[turn],
            recv_sem=bwd_recv.at[turn, own_chunk],
            device_id=(layer, base + target),
            device_id_type=MESH,
        )

    def backward_own(turn):
        return pltpu.make_async_copy(
            bwd_src.at[turn, here], bwd_rcv.at[turn, *piece(here)], bwd_recv.at[turn, own_chunk]
        )

    def peer(offset):
        return lax.rem(here + offset, group)

    def all_of(ref, sem):
        pltpu.make_async_copy(ref, ref, sem).wait()

    def damping():
        all_of(dec_rcv, dec_recv)
        for j in range(group):
            dec_all[j] = jnp.broadcast_to(dec_rcv[j], (8, width))
        right = jnp.ones((8, width), F32)
        for j in range(group):
            right = right * dec_all[j]
            cum[j] = right
        left = jnp.ones((8, width), F32)
        for j in range(group - 1, -1, -1):
            left = left * dec_all[j]
            cum[j] = jnp.where(run == 1, cum[j], left)

    def part(b):
        return pl.ds(b * part_rows, part_rows)

    def third(b):
        return 3 * b // PARTS

    def relay_part(b):
        return relay.at[part(RELAYED.index(b))]

    def ship_copy(b, source):
        relayed = b in RELAYED
        return pltpu.make_async_remote_copy(
            src_ref=source.at[part(b)],
            dst_ref=relay_part(b) if relayed else stage.at[2, part(b)],
            send_sem=part_send,
            recv_sem=relay_recv.at[RELAYED.index(b)] if relayed else part_recv.at[third(b)],
            device_id=(relay_by if relayed else neighbour, cell),
            device_id_type=MESH,
        )

    def ship(*parts):
        for turn, other in enumerate((up_hbm, down_hbm)):

            @pl.when(jnp.logical_and(inner, way == turn))
            def _():
                for b in parts:
                    ship_copy(b, other).start()

    def hand_on(*parts):
        @pl.when(rank < 2)
        def _():
            for b in parts:
                all_of(relay_part(b), relay_recv.at[RELAYED.index(b)])
                pltpu.make_async_remote_copy(
                    src_ref=relay_part(b),
                    dst_ref=stage.at[2, part(b)],
                    send_sem=part_send,
                    recv_sem=part_recv.at[third(b)],
                    device_id=(across, cell),
                    device_id_type=MESH,
                ).start()

    def own_sweep(turn, meanwhile):
        all_of(fwd_rcv.at[turn], fwd_recv.at[turn])
        right = jnp.zeros((8, width), F32)
        left = jnp.zeros((8, width), F32)
        for j in range(group):
            right = dec_all[j] * right + fwd_rcv[turn, j]
            bwd_src[turn, j] = right
            back = group - 1 - j
            left = dec_all[back] * left + fwd_rcv[turn, back]
            lefts[back] = left
        car_src[turn] = jnp.where(run == 0, right, left)
        carry_copy(turn).start()
        meanwhile()
        carry_copy(turn).wait_recv()
        carry = car_rcv[turn]
        for j in range(group):
            bwd_src[turn, j] = bwd_src[turn, j] + lefts[j] + cum[j] * carry
        for offset in far_first(group):
            backward_copy(turn, peer(offset)).start()
        backward_own(turn).start()

    def chunk_rows(index):
        return pl.ds(index * chunk, chunk)

    def collected(turn, index):
        rows = chunk_rows(index)
        all_of(bwd_rcv.at[turn, rows], bwd_recv.at[turn, index])
        return anchor[rows, :] + lateral_weight * bwd_rcv[turn, rows, :]

    def prepare_main():
        @pl.when(rank > 0)
        def _():
            operator_load(down_hbm, 1).wait()
            for b in range(3):
                prepare(1, b, dep_high.at[0], dep_low.at[0])

    def prepare_other(b):
        all_of(stage.at[2, pl.ds(b * block, block)], part_recv.at[b])
        prepare(2, b, dep_high.at[1], dep_low.at[1])

    def first_meanwhile():
        ship(2, 3, 4)

        @pl.when(rank == 1)
        def _():
            operator_load(down_hbm, 2).wait()
            for b in range(3):
                prepare(2, b, dep_high.at[1], dep_low.at[1])

    def second_meanwhile():
        ship(7, 8, 9)
        hand_on(6)

        @pl.when(inner)
        def _():
            prepare_other(0)

    ship(1, 0)
    prepare_main()
    damping()
    own_sweep(0, first_meanwhile)
    ship(5, 6)
    hand_on(1)
    for index in range(CHUNKS):
        rows = chunk_rows(index)
        fwd_src[1, rows, :] = product(collected(0, index), lat_high[...], lat_low[...])
        send_forward(1, index)
    hand_on(5)
    own_sweep(1, second_meanwhile)
    ship(10, 11)

    @pl.when(inner)
    def _():
        prepare_other(1)

    def depth_chunk(k):
        return pl.ds(pl.multiple_of(k * depth_rows, 8), depth_rows)

    def depth_copy(source, k, send, slot, target):
        rows = depth_chunk(k)
        return pltpu.make_async_remote_copy(
            src_ref=source.at[rows],
            dst_ref=dep_rcv.at[slot, rows],
            send_sem=dep_send.at[send],
            recv_sem=dep_recv.at[slot, k],
            device_id=(target, cell),
            device_id_type=MESH,
        )

    def arrived(slot, k):
        ref = dep_rcv.at[slot, depth_chunk(k)]
        pltpu.make_async_copy(ref, ref, dep_recv.at[slot, k]).wait()

    def mate_copy(index):
        rows = chunk_rows(index)
        return pltpu.make_async_remote_copy(
            src_ref=smooth.at[rows],
            dst_ref=mate.at[rows],
            send_sem=mate_send,
            recv_sem=mate_recv,
            device_id=(neighbour, cell),
            device_id_type=MESH,
        )

    for index in range(CHUNKS):
        rows = chunk_rows(index)
        smooth[rows, :] = collected(1, index)

        @pl.when(rank == 0)
        def _():
            for k in range(index * per_chunk, (index + 1) * per_chunk):
                depth_copy(smooth, k, 0, 0, chain_to).start()

        @pl.when(inner)
        def _():
            mate_copy(index).start()

    hand_on(10, 11)

    def applied(c, which):
        return product(c, dep_high[which], dep_low[which])

    @pl.when(rank == 1)
    def _():
        @pl.loop(0, DEPTH_CHUNKS)
        def _(k):
            rows = depth_chunk(k)
            arrived(0, k)
            dep_src[0, rows, :] = smooth[rows, :] + applied(dep_rcv[0, rows, :], 0)
            depth_copy(dep_src.at[0], k, 0, 0, chain_to).start()
            out_ref[rows, :] = smooth[rows, :] + depth_weight * dep_rcv[0, rows, :]

        @pl.loop(0, DEPTH_CHUNKS)
        def _(k):
            rows = depth_chunk(k)
            arrived(1, k)
            dep_src[1, rows, :] = smooth[rows, :] + applied(dep_rcv[1, rows, :], 1)
            depth_copy(dep_src.at[1], k, 1, 1, back_to).start()
            out_ref[rows, :] = out_ref[rows, :] + depth_weight * dep_rcv[1, rows, :]

    @pl.when(rank == 0)
    def _():
        @pl.loop(0, DEPTH_CHUNKS)
        def _(k):
            rows = depth_chunk(k)
            arrived(1, k)
            out_ref[rows, :] = smooth[rows, :] + depth_weight * dep_rcv[1, rows, :]

    @pl.when(inner)
    def _():
        prepare_other(2)
        all_of(mate, mate_recv)

        @pl.loop(0, DEPTH_CHUNKS)
        def _(k):
            rows = depth_chunk(k)
            arrived(0, k)
            near = smooth[rows, :] + applied(dep_rcv[0, rows, :], 0)
            dep_src[0, rows, :] = near
            dep_src[1, rows, :] = mate[rows, :] + applied(near, 1)
            depth_copy(dep_src.at[1], k, 0, chain_slot, chain_to).start()
            depth_copy(dep_src.at[0], k, 1, 1, neighbour).start()
            out_ref[rows, :] = smooth[rows, :] + depth_weight * dep_rcv[0, rows, :]

        @pl.loop(0, DEPTH_CHUNKS)
        def _(k):
            rows = depth_chunk(k)
            arrived(1, k)
            out_ref[rows, :] = out_ref[rows, :] + depth_weight * dep_rcv[1, rows, :]

    peers = pl.ds(0, group - 1)
    for turn in range(PASSES):
        all_of(fwd_rcv.at[turn, peers], fwd_send.at[turn])
        all_of(bwd_src.at[turn, peers], bwd_send.at[turn])
        all_of(car_src.at[turn], car_send.at[turn])
    all_of(dec_rcv.at[peers], dec_send)
    all_of(smooth, dep_send.at[0])

    @pl.when(rank > 0)
    def _():
        all_of(smooth, dep_send.at[1])

    @pl.when(inner)
    def _():
        all_of(smooth, mate_send)
        all_of(stage.at[0], part_send)

    @pl.when(rank < 2)
    def _():
        all_of(relay, part_send)


def shards(source, rate, lat_op, down_op, up_op):
    order, columns = source.shape[2:]
    layers = lax.axis_size("depth")
    cells = lax.axis_size("lat")
    group = cells // 2
    width = order // 2
    any_space = pl.BlockSpec(memory_space=pl.ANY)
    vmem = pltpu.VMEM
    dma = pltpu.SemaphoreType.DMA
    traces = pl.pallas_call(
        functools.partial(kernel, layers, cells),
        name="sweeps",
        out_shape=jax.ShapeDtypeStruct((columns, order), F32),
        in_specs=[any_space] * 5,
        out_specs=pl.BlockSpec(memory_space=pltpu.VMEM),
        scratch_shapes=[
            vmem((columns, order), F32),
            vmem((1, order), F32),
            vmem((1, order), F32),
            vmem((3, order, order), F32),
            vmem((order, order), BF16),
            vmem((order, order), BF16),
            vmem((2, order, order), BF16),
            vmem((2, order, order), BF16),
            vmem((PASSES, columns, order), F32),
            vmem((PASSES, group, 8, width), F32),
            vmem((PASSES, 8, width), F32),
            vmem((PASSES, 8, width), F32),
            vmem((PASSES, group, 8, width), F32),
            vmem((PASSES, columns, order), F32),
            vmem((group, 1, width), F32),
            vmem((group, 8, width), F32),
            vmem((group, 8, width), F32),
            vmem((group, 8, width), F32),
            vmem((columns, order), F32),
            vmem((2, columns, order), F32),
            vmem((2, columns, order), F32),
            vmem((columns, order), F32),
            vmem((len(RELAYED) * (order // PARTS), order), F32),
            dma((7,)),
            dma,
            dma,
            dma((PASSES,)),
            dma((PASSES,)),
            dma((PASSES,)),
            dma((PASSES,)),
            dma((PASSES,)),
            dma((PASSES, CHUNKS)),
            dma((2,)),
            dma((2, DEPTH_CHUNKS)),
            dma,
            dma,
            dma,
            dma((3,)),
            dma((len(RELAYED),)),
        ],
        compiler_params=pltpu.CompilerParams(
            collective_id=0, has_side_effects=True, vmem_limit_bytes=56200000
        ),
    )(
        source.reshape(order, columns).T,
        rate.reshape(1, order),
        lat_op.reshape(order, order),
        down_op.reshape(order, order),
        up_op.reshape(order, order),
    )
    return traces.T.reshape(1, 1, order, columns)


def solution(mesh):
    spec = P("depth", "lat", None, None)
    in_specs = (spec, P("depth", "lat", None), spec, spec, spec)
    return jax.shard_map(shards, mesh=mesh, in_specs=in_specs, out_specs=spec, check_vma=False)
```

```python
import functools

import jax
import jax.numpy as jnp
from jax import lax
from jax.experimental import pallas as pl
from jax.experimental.pallas import tpu as pltpu
from jax.sharding import PartitionSpec as P

PASSES = 2
CHUNKS = 2
DEPTH_CHUNKS = 4
PARTS = 12
RELAYED = (1, 5, 6, 10, 11,)

lateral_weight = 0.1
depth_weight = 0.25

MESH = pl.DeviceIdType.MESH
F32 = jnp.float32
BF16 = jnp.bfloat16


def split(x):
    high = x.astype(BF16)
    return high, (x - high.astype(F32)).astype(BF16)


def product(x, high, low):
    rows = x.shape[0]
    x_high, x_low = split(x)
    both = jnp.dot(jnp.concatenate([x_high, x_low], axis=0), high, preferred_element_type=F32)
    return both[:rows] + (both[rows:] + jnp.dot(x_high, low, preferred_element_type=F32))


def kernel(
    layers,
    cells,
    src_hbm,
    rate_hbm,
    lat_hbm,
    down_hbm,
    up_hbm,
    out_ref,
    anchor,
    rate,
    decay,
    stage,
    lat_high,
    lat_low,
    dep_high,
    dep_low,
    fwd_src,
    fwd_rcv,
    car_src,
    car_rcv,
    bwd_src,
    bwd_rcv,
    dec_rcv,
    dec_all,
    cum,
    lefts,
    smooth,
    dep_src,
    dep_rcv,
    mate,
    relay,
    load_sem,
    dec_send,
    dec_recv,
    fwd_send,
    fwd_recv,
    car_send,
    car_recv,
    bwd_send,
    bwd_recv,
    dep_send,
    dep_recv,
    mate_send,
    mate_recv,
    part_send,
    part_recv,
    relay_recv,
):
    columns, order = anchor.shape
    group = cells // 2
    width = order // 2
    chunk = columns // CHUNKS
    owners = group // CHUNKS
    depth_rows = columns // DEPTH_CHUNKS
    per_chunk = DEPTH_CHUNKS // CHUNKS
    block = order // 3
    part_rows = order // PARTS

    layer = lax.axis_index("depth")
    cell = lax.axis_index("lat")
    run = cell // group
    here = lax.rem(cell, group)
    place_in_chunk = here // CHUNKS
    own_chunk = lax.rem(here, CHUNKS)
    base = run * group

    way = jnp.where(jnp.logical_or(layer == 3, layer >= 5), 1, 0)
    rank = jnp.where(way == 0, layer, layers - 1 - layer)
    inner = rank >= 2
    neighbour = layer + 1 - 2 * lax.rem(layer, 2)
    quad = (layer // 4) * 4
    across = jnp.where(layer < 4, layer + 2, layer - 2)
    relay_by = jnp.where(layer < 4, 3 - layer, 11 - layer)
    after = rank + jnp.where(rank < 2, 1, 2)
    chain_to = jnp.where(way == 0, after, layers - 1 - after)
    chain_slot = jnp.where(rank == 4, 1, 0)
    back_to = layer - 1 + 2 * way

    def operator_load(own, slot):
        return pltpu.make_async_copy(own, stage.at[slot], load_sem.at[4 + slot])

    def load_operators():
        for turn, (main, other) in enumerate(((down_hbm, up_hbm), (up_hbm, down_hbm))):

            @pl.when(jnp.logical_and(way == turn, rank > 0))
            def _():
                operator_load(main, 1).start()

            @pl.when(jnp.logical_and(way == turn, rank == 1))
            def _():
                operator_load(other, 2).start()

    loads = [
        pltpu.make_async_copy(src_hbm, anchor, load_sem.at[0]),
        pltpu.make_async_copy(rate_hbm, rate, load_sem.at[1]),
    ]
    for b in range(3):
        rows = pl.ds(b * block, block)
        loads.append(pltpu.make_async_copy(lat_hbm.at[rows], stage.at[0, rows], load_sem.at[2 + b]))
    for load in loads:
        load.start()

    barrier = pltpu.get_barrier_semaphore()
    for offset in range(1, group):
        pl.semaphore_signal(
            barrier, inc=1, device_id=(layer, base + lax.rem(here + offset, group)), device_id_type=MESH
        )
    other_run = (1 - run) * group + here
    pl.semaphore_signal(barrier, inc=1, device_id=(layer, other_run), device_id_type=MESH)

    for offset in range(1, 4):
        mate_layer = quad + lax.rem(layer - quad + offset, 4)
        pl.semaphore_signal(barrier, inc=1, device_id=(mate_layer, cell), device_id_type=MESH)

    @pl.when(inner)
    def _():
        pl.semaphore_signal(barrier, inc=1, device_id=(across, cell), device_id_type=MESH)

    def prepare(which, b, high, low):
        rows = pl.ds(b * block, block)
        turned = stage[which, rows, :].T
        top, rest = split(turned)
        high[:, rows] = top
        low[:, rows] = rest

    loads[0].wait()
    for b in range(3):
        rows = pl.ds(b * block, block)
        loads[2 + b].wait()
        prepare(0, b, lat_high, lat_low)
        fwd_src[0, :, rows] = product(anchor[...], lat_high[:, rows], lat_low[:, rows])
    load_operators()
    loads[1].wait()
    decay[...] = jnp.exp(-rate[...])

    pl.semaphore_wait(barrier, group + 3 + jnp.where(inner, 1, 0))

    def far_first(count):
        return sorted(range(1, count), key=lambda step: -min(step, count - step))

    def piece(owner):
        part = owner // CHUNKS
        return (
            pl.ds(pl.multiple_of(lax.rem(owner, CHUNKS) * chunk + 8 * (part // 2), 8), 8),
            pl.ds(pl.multiple_of(lax.rem(part, 2) * width, width), width),
        )

    def forward_copy(turn, owner):
        return pltpu.make_async_remote_copy(
            src_ref=fwd_src.at[turn, *piece(owner)],
            dst_ref=fwd_rcv.at[turn, here],
            send_sem=fwd_send.at[turn],
            recv_sem=fwd_recv.at[turn],
            device_id=(layer, base + owner),
            device_id_type=MESH,
        )

    def forward_own(turn):
        return pltpu.make_async_copy(
            fwd_src.at[turn, *piece(here)], fwd_rcv.at[turn, here], fwd_recv.at[turn]
        )

    def decay_copy(owner):
        return pltpu.make_async_remote_copy(
            src_ref=decay.at[:, piece(owner)[1]],
            dst_ref=dec_rcv.at[here],
            send_sem=dec_send,
            recv_sem=dec_recv,
            device_id=(layer, base + owner),
            device_id_type=MESH,
        )

    def decay_own():
        return pltpu.make_async_copy(decay.at[:, piece(here)[1]], dec_rcv.at[here], dec_recv)

    def owner_of(index, offset):
        return index + CHUNKS * lax.rem(place_in_chunk + offset, owners)

    def send_forward(turn, index):
        for offset in far_first(owners):
            if turn == 0:
                decay_copy(owner_of(index, offset)).start()
            forward_copy(turn, owner_of(index, offset)).start()

        @pl.when(own_chunk != index)
        def _():
            if turn == 0:
                decay_copy(owner_of(index, 0)).start()
            forward_copy(turn, owner_of(index, 0)).start()

        @pl.when(own_chunk == index)
        def _():
            if turn == 0:
                decay_own().start()
            forward_own(turn).start()

    for index in range(CHUNKS):
        send_forward(0, index)

    def carry_copy(turn):
        return pltpu.make_async_remote_copy(
            src_ref=car_src.at[turn],
            dst_ref=car_rcv.at[turn],
            send_sem=car_send.at[turn],
            recv_sem=car_recv.at[turn],
            device_id=(layer, other_run),
            device_id_type=MESH,
        )

    def backward_copy(turn, target):
        return pltpu.make_async_remote_copy(
            src_ref=bwd_src.at[turn, target],
            dst_ref=bwd_rcv.at[turn, *piece(here)],
            send_sem=bwd_send.at[turn],
            recv_sem=bwd_recv.at[turn, own_chunk],
            device_id=(layer, base + target),
            device_id_type=MESH,
        )

    def backward_own(turn):
        return pltpu.make_async_copy(
            bwd_src.at[turn, here], bwd_rcv.at[turn, *piece(here)], bwd_recv.at[turn, own_chunk]
        )

    def peer(offset):
        return lax.rem(here + offset, group)

    def all_of(ref, sem):
        pltpu.make_async_copy(ref, ref, sem).wait()

    def damping():
        all_of(dec_rcv, dec_recv)
        for j in range(group):
            dec_all[j] = jnp.broadcast_to(dec_rcv[j], (8, width))
        right = jnp.ones((8, width), F32)
        for j in range(group):
            right = right * dec_all[j]
            cum[j] = right
        left = jnp.ones((8, width), F32)
        for j in range(group - 1, -1, -1):
            left = left * dec_all[j]
            cum[j] = jnp.where(run == 1, cum[j], left)

    def part(b):
        return pl.ds(b * part_rows, part_rows)

    def third(b):
        return 3 * b // PARTS

    def relay_part(b):
        return relay.at[part(RELAYED.index(b))]

    def ship_copy(b, source):
        relayed = b in RELAYED
        return pltpu.make_async_remote_copy(
            src_ref=source.at[part(b)],
            dst_ref=relay_part(b) if relayed else stage.at[2, part(b)],
            send_sem=part_send,
            recv_sem=relay_recv.at[RELAYED.index(b)] if relayed else part_recv.at[third(b)],
            device_id=(relay_by if relayed else neighbour, cell),
            device_id_type=MESH,
        )

    def ship(*parts):
        for turn, other in enumerate((up_hbm, down_hbm)):

            @pl.when(jnp.logical_and(inner, way == turn))
            def _():
                for b in parts:
                    ship_copy(b, other).start()

    def hand_on(*parts):
        @pl.when(rank < 2)
        def _():
            for b in parts:
                all_of(relay_part(b), relay_recv.at[RELAYED.index(b)])
                pltpu.make_async_remote_copy(
                    src_ref=relay_part(b),
                    dst_ref=stage.at[2, part(b)],
                    send_sem=part_send,
                    recv_sem=part_recv.at[third(b)],
                    device_id=(across, cell),
                    device_id_type=MESH,
                ).start()

    def own_sweep(turn, meanwhile):
        all_of(fwd_rcv.at[turn], fwd_recv.at[turn])
        right = jnp.zeros((8, width), F32)
        left = jnp.zeros((8, width), F32)
        for j in range(group):
            right = dec_all[j] * right + fwd_rcv[turn, j]
            bwd_src[turn, j] = right
            back = group - 1 - j
            left = dec_all[back] * left + fwd_rcv[turn, back]
            lefts[back] = left
        car_src[turn] = jnp.where(run == 0, right, left)
        carry_copy(turn).start()
        meanwhile()
        carry_copy(turn).wait_recv()
        carry = car_rcv[turn]
        for j in range(group):
            bwd_src[turn, j] = bwd_src[turn, j] + lefts[j] + cum[j] * carry
        for offset in far_first(group):
            backward_copy(turn, peer(offset)).start()
        backward_own(turn).start()

    def chunk_rows(index):
        return pl.ds(index * chunk, chunk)

    def collected(turn, index):
        rows = chunk_rows(index)
        all_of(bwd_rcv.at[turn, rows], bwd_recv.at[turn, index])
        return anchor[rows, :] + lateral_weight * bwd_rcv[turn, rows, :]

    def prepare_main():
        @pl.when(rank > 0)
        def _():
            operator_load(down_hbm, 1).wait()
            for b in range(3):
                prepare(1, b, dep_high.at[0], dep_low.at[0])

    def prepare_other(b):
        all_of(stage.at[2, pl.ds(b * block, block)], part_recv.at[b])
        prepare(2, b, dep_high.at[1], dep_low.at[1])

    def first_meanwhile():
        ship(2, 3, 4, 7)

        @pl.when(rank == 1)
        def _():
            operator_load(down_hbm, 2).wait()
            for b in range(3):
                prepare(2, b, dep_high.at[1], dep_low.at[1])

    def second_meanwhile():
        ship(8, 9)
        hand_on(6)

        @pl.when(inner)
        def _():
            prepare_other(0)

    ship(1, 0)
    prepare_main()
    damping()
    own_sweep(0, first_meanwhile)
    ship(5, 6)
    hand_on(1)
    for index in range(CHUNKS):
        rows = chunk_rows(index)
        fwd_src[1, rows, :] = product(collected(0, index), lat_high[...], lat_low[...])
        send_forward(1, index)
    ship(10)
    hand_on(5)
    own_sweep(1, second_meanwhile)
    ship(11)
    hand_on(10)

    @pl.when(inner)
    def _():
        prepare_other(1)

    def depth_chunk(k):
        return pl.ds(pl.multiple_of(k * depth_rows, 8), depth_rows)

    def depth_copy(source, k, send, slot, target):
        rows = depth_chunk(k)
        return pltpu.make_async_remote_copy(
            src_ref=source.at[rows],
            dst_ref=dep_rcv.at[slot, rows],
            send_sem=dep_send.at[send],
            recv_sem=dep_recv.at[slot, k],
            device_id=(target, cell),
            device_id_type=MESH,
        )

    def arrived(slot, k):
        ref = dep_rcv.at[slot, depth_chunk(k)]
        pltpu.make_async_copy(ref, ref, dep_recv.at[slot, k]).wait()

    def mate_copy(index):
        rows = chunk_rows(index)
        return pltpu.make_async_remote_copy(
            src_ref=smooth.at[rows],
            dst_ref=mate.at[rows],
            send_sem=mate_send,
            recv_sem=mate_recv.at[index],
            device_id=(neighbour, cell),
            device_id_type=MESH,
        )

    for index in range(CHUNKS):
        rows = chunk_rows(index)
        smooth[rows, :] = collected(1, index)

        @pl.when(rank == 0)
        def _():
            for k in range(index * per_chunk, (index + 1) * per_chunk):
                depth_copy(smooth, k, 0, 0, chain_to).start()

        @pl.when(inner)
        def _():
            mate_copy(index).start()

    hand_on(11)

    def applied(c, which):
        return product(c, dep_high[which], dep_low[which])

    @pl.when(rank == 1)
    def _():
        @pl.loop(0, DEPTH_CHUNKS)
        def _(k):
            rows = depth_chunk(k)
            arrived(0, k)
            dep_src[0, rows, :] = smooth[rows, :] + applied(dep_rcv[0, rows, :], 0)
            depth_copy(dep_src.at[0], k, 0, 0, chain_to).start()
            out_ref[rows, :] = smooth[rows, :] + depth_weight * dep_rcv[0, rows, :]

        @pl.loop(0, DEPTH_CHUNKS)
        def _(k):
            rows = depth_chunk(k)
            arrived(1, k)
            dep_src[1, rows, :] = smooth[rows, :] + applied(dep_rcv[1, rows, :], 1)
            depth_copy(dep_src.at[1], k, 1, 1, back_to).start()
            out_ref[rows, :] = out_ref[rows, :] + depth_weight * dep_rcv[1, rows, :]

    @pl.when(rank == 0)
    def _():
        @pl.loop(0, DEPTH_CHUNKS)
        def _(k):
            rows = depth_chunk(k)
            arrived(1, k)
            out_ref[rows, :] = smooth[rows, :] + depth_weight * dep_rcv[1, rows, :]

    @pl.when(inner)
    def _():
        prepare_other(2)
        @pl.loop(0, DEPTH_CHUNKS)
        def _(k):
            rows = depth_chunk(k)
            arrived(0, k)
            near = smooth[rows, :] + applied(dep_rcv[0, rows, :], 0)
            dep_src[0, rows, :] = near
            for index in range(CHUNKS):

                @pl.when(k == index * per_chunk)
                def _():
                    all_of(mate.at[chunk_rows(index)], mate_recv.at[index])

            dep_src[1, rows, :] = mate[rows, :] + applied(near, 1)
            depth_copy(dep_src.at[1], k, 0, chain_slot, chain_to).start()
            depth_copy(dep_src.at[0], k, 1, 1, neighbour).start()
            out_ref[rows, :] = smooth[rows, :] + depth_weight * dep_rcv[0, rows, :]

        @pl.loop(0, DEPTH_CHUNKS)
        def _(k):
            rows = depth_chunk(k)
            arrived(1, k)
            out_ref[rows, :] = out_ref[rows, :] + depth_weight * dep_rcv[1, rows, :]

    peers = pl.ds(0, group - 1)
    for turn in range(PASSES):
        all_of(fwd_rcv.at[turn, peers], fwd_send.at[turn])
        all_of(bwd_src.at[turn, peers], bwd_send.at[turn])
        all_of(car_src.at[turn], car_send.at[turn])
    all_of(dec_rcv.at[peers], dec_send)
    all_of(smooth, dep_send.at[0])

    @pl.when(rank > 0)
    def _():
        all_of(smooth, dep_send.at[1])

    @pl.when(inner)
    def _():
        all_of(smooth, mate_send)
        all_of(stage.at[0], part_send)

    @pl.when(rank < 2)
    def _():
        all_of(relay, part_send)


def shards(source, rate, lat_op, down_op, up_op):
    order, columns = source.shape[2:]
    layers = lax.axis_size("depth")
    cells = lax.axis_size("lat")
    group = cells // 2
    width = order // 2
    any_space = pl.BlockSpec(memory_space=pl.ANY)
    vmem = pltpu.VMEM
    dma = pltpu.SemaphoreType.DMA
    traces = pl.pallas_call(
        functools.partial(kernel, layers, cells),
        name="sweeps",
        out_shape=jax.ShapeDtypeStruct((columns, order), F32),
        in_specs=[any_space] * 5,
        out_specs=pl.BlockSpec(memory_space=pltpu.VMEM),
        scratch_shapes=[
            vmem((columns, order), F32),
            vmem((1, order), F32),
            vmem((1, order), F32),
            vmem((3, order, order), F32),
            vmem((order, order), BF16),
            vmem((order, order), BF16),
            vmem((2, order, order), BF16),
            vmem((2, order, order), BF16),
            vmem((PASSES, columns, order), F32),
            vmem((PASSES, group, 8, width), F32),
            vmem((PASSES, 8, width), F32),
            vmem((PASSES, 8, width), F32),
            vmem((PASSES, group, 8, width), F32),
            vmem((PASSES, columns, order), F32),
            vmem((group, 1, width), F32),
            vmem((group, 8, width), F32),
            vmem((group, 8, width), F32),
            vmem((group, 8, width), F32),
            vmem((columns, order), F32),
            vmem((2, columns, order), F32),
            vmem((2, columns, order), F32),
            vmem((columns, order), F32),
            vmem((len(RELAYED) * (order // PARTS), order), F32),
            dma((7,)),
            dma,
            dma,
            dma((PASSES,)),
            dma((PASSES,)),
            dma((PASSES,)),
            dma((PASSES,)),
            dma((PASSES,)),
            dma((PASSES, CHUNKS)),
            dma((2,)),
            dma((2, DEPTH_CHUNKS)),
            dma,
            dma((CHUNKS,)),
            dma,
            dma((3,)),
            dma((len(RELAYED),)),
        ],
        compiler_params=pltpu.CompilerParams(
            collective_id=0, has_side_effects=True, vmem_limit_bytes=56200000
        ),
    )(
        source.reshape(order, columns).T,
        rate.reshape(1, order),
        lat_op.reshape(order, order),
        down_op.reshape(order, order),
        up_op.reshape(order, order),
    )
    return traces.T.reshape(1, 1, order, columns)


def solution(mesh):
    spec = P("depth", "lat", None, None)
    in_specs = (spec, P("depth", "lat", None), spec, spec, spec)
    return jax.shard_map(shards, mesh=mesh, in_specs=in_specs, out_specs=spec, check_vma=False)
```

```python
import functools

import jax
import jax.numpy as jnp
from jax import lax
from jax.experimental import pallas as pl
from jax.experimental.pallas import tpu as pltpu
from jax.sharding import PartitionSpec as P

PASSES = 2
CHUNKS = 2
DEPTH_CHUNKS = 4
PARTS = 12
RELAYED = (1, 5, 6, 10, 11,)

lateral_weight = 0.1
depth_weight = 0.25

MESH = pl.DeviceIdType.MESH
F32 = jnp.float32
BF16 = jnp.bfloat16


def split(x):
    high = x.astype(BF16)
    return high, (x - high.astype(F32)).astype(BF16)


def product(x, high, low):
    rows = x.shape[0]
    x_high, x_low = split(x)
    both = jnp.dot(jnp.concatenate([x_high, x_low], axis=0), high, preferred_element_type=F32)
    return both[:rows] + (both[rows:] + jnp.dot(x_high, low, preferred_element_type=F32))


def kernel(
    layers,
    cells,
    src_hbm,
    rate_hbm,
    lat_hbm,
    down_hbm,
    up_hbm,
    out_ref,
    anchor,
    rate,
    decay,
    stage,
    lat_high,
    lat_low,
    dep_high,
    dep_low,
    fwd_src,
    fwd_rcv,
    car_src,
    car_rcv,
    bwd_src,
    bwd_rcv,
    dec_rcv,
    dec_all,
    cum,
    lefts,
    smooth,
    dep_src,
    dep_rcv,
    mate,
    relay,
    load_sem,
    dec_send,
    dec_recv,
    fwd_send,
    fwd_recv,
    car_send,
    car_recv,
    bwd_send,
    bwd_recv,
    dep_send,
    dep_recv,
    mate_send,
    mate_recv,
    part_send,
    part_recv,
    relay_recv,
):
    columns, order = anchor.shape
    group = cells // 2
    width = order // 2
    chunk = columns // CHUNKS
    owners = group // CHUNKS
    depth_rows = columns // DEPTH_CHUNKS
    per_chunk = DEPTH_CHUNKS // CHUNKS
    block = order // 3
    part_rows = order // PARTS

    layer = lax.axis_index("depth")
    cell = lax.axis_index("lat")
    run = cell // group
    here = lax.rem(cell, group)
    place_in_chunk = here // CHUNKS
    own_chunk = lax.rem(here, CHUNKS)
    base = run * group

    way = jnp.where(jnp.logical_or(layer == 3, layer >= 5), 1, 0)
    rank = jnp.where(way == 0, layer, layers - 1 - layer)
    inner = rank >= 2
    neighbour = layer + 1 - 2 * lax.rem(layer, 2)
    quad = (layer // 4) * 4
    across = jnp.where(layer < 4, layer + 2, layer - 2)
    relay_by = jnp.where(layer < 4, 3 - layer, 11 - layer)
    after = rank + jnp.where(rank < 2, 1, 2)
    chain_to = jnp.where(way == 0, after, layers - 1 - after)
    chain_slot = jnp.where(rank == 4, 1, 0)
    back_to = layer - 1 + 2 * way

    def operator_load(own, slot):
        return pltpu.make_async_copy(own, stage.at[slot], load_sem.at[4 + slot])

    def load_operators():
        for turn, (main, other) in enumerate(((down_hbm, up_hbm), (up_hbm, down_hbm))):

            @pl.when(jnp.logical_and(way == turn, rank > 0))
            def _():
                operator_load(main, 1).start()

            @pl.when(jnp.logical_and(way == turn, rank == 1))
            def _():
                operator_load(other, 2).start()

    loads = [
        pltpu.make_async_copy(src_hbm, anchor, load_sem.at[0]),
        pltpu.make_async_copy(rate_hbm, rate, load_sem.at[1]),
    ]
    for b in range(3):
        rows = pl.ds(b * block, block)
        loads.append(pltpu.make_async_copy(lat_hbm.at[rows], stage.at[0, rows], load_sem.at[2 + b]))
    for load in loads:
        load.start()

    barrier = pltpu.get_barrier_semaphore()
    for offset in range(1, group):
        pl.semaphore_signal(
            barrier, inc=1, device_id=(layer, base + lax.rem(here + offset, group)), device_id_type=MESH
        )
    other_run = (1 - run) * group + here
    pl.semaphore_signal(barrier, inc=1, device_id=(layer, other_run), device_id_type=MESH)

    for offset in range(1, 4):
        mate_layer = quad + lax.rem(layer - quad + offset, 4)
        pl.semaphore_signal(barrier, inc=1, device_id=(mate_layer, cell), device_id_type=MESH)

    @pl.when(inner)
    def _():
        pl.semaphore_signal(barrier, inc=1, device_id=(across, cell), device_id_type=MESH)

    def prepare(which, b, high, low):
        rows = pl.ds(b * block, block)
        turned = stage[which, rows, :].T
        top, rest = split(turned)
        high[:, rows] = top
        low[:, rows] = rest

    loads[0].wait()
    for b in range(3):
        rows = pl.ds(b * block, block)
        loads[2 + b].wait()
        prepare(0, b, lat_high, lat_low)
        fwd_src[0, :, rows] = product(anchor[...], lat_high[:, rows], lat_low[:, rows])
    load_operators()
    loads[1].wait()
    decay[...] = jnp.exp(-rate[...])

    pl.semaphore_wait(barrier, group + 3 + jnp.where(inner, 1, 0))

    def far_first(count):
        return sorted(range(1, count), key=lambda step: -min(step, count - step))

    def piece(owner):
        part = owner // CHUNKS
        return (
            pl.ds(pl.multiple_of(lax.rem(owner, CHUNKS) * chunk + 8 * (part // 2), 8), 8),
            pl.ds(pl.multiple_of(lax.rem(part, 2) * width, width), width),
        )

    def forward_copy(turn, owner):
        return pltpu.make_async_remote_copy(
            src_ref=fwd_src.at[turn, *piece(owner)],
            dst_ref=fwd_rcv.at[turn, here],
            send_sem=fwd_send.at[turn],
            recv_sem=fwd_recv.at[turn],
            device_id=(layer, base + owner),
            device_id_type=MESH,
        )

    def forward_own(turn):
        return pltpu.make_async_copy(
            fwd_src.at[turn, *piece(here)], fwd_rcv.at[turn, here], fwd_recv.at[turn]
        )

    def decay_copy(owner):
        return pltpu.make_async_remote_copy(
            src_ref=decay.at[:, piece(owner)[1]],
            dst_ref=dec_rcv.at[here],
            send_sem=dec_send,
            recv_sem=dec_recv,
            device_id=(layer, base + owner),
            device_id_type=MESH,
        )

    def decay_own():
        return pltpu.make_async_copy(decay.at[:, piece(here)[1]], dec_rcv.at[here], dec_recv)

    def owner_of(index, offset):
        return index + CHUNKS * lax.rem(place_in_chunk + offset, owners)

    def send_forward(turn, index):
        for offset in far_first(owners):
            if turn == 0:
                decay_copy(owner_of(index, offset)).start()
            forward_copy(turn, owner_of(index, offset)).start()

        @pl.when(own_chunk != index)
        def _():
            if turn == 0:
                decay_copy(owner_of(index, 0)).start()
            forward_copy(turn, owner_of(index, 0)).start()

        @pl.when(own_chunk == index)
        def _():
            if turn == 0:
                decay_own().start()
            forward_own(turn).start()

    for index in range(CHUNKS):
        send_forward(0, index)

    def carry_copy(turn):
        return pltpu.make_async_remote_copy(
            src_ref=car_src.at[turn],
            dst_ref=car_rcv.at[turn],
            send_sem=car_send.at[turn],
            recv_sem=car_recv.at[turn],
            device_id=(layer, other_run),
            device_id_type=MESH,
        )

    def backward_copy(turn, target):
        return pltpu.make_async_remote_copy(
            src_ref=bwd_src.at[turn, target],
            dst_ref=bwd_rcv.at[turn, *piece(here)],
            send_sem=bwd_send.at[turn],
            recv_sem=bwd_recv.at[turn, own_chunk],
            device_id=(layer, base + target),
            device_id_type=MESH,
        )

    def backward_own(turn):
        return pltpu.make_async_copy(
            bwd_src.at[turn, here], bwd_rcv.at[turn, *piece(here)], bwd_recv.at[turn, own_chunk]
        )

    def peer(offset):
        return lax.rem(here + offset, group)

    def all_of(ref, sem):
        pltpu.make_async_copy(ref, ref, sem).wait()

    def damping():
        all_of(dec_rcv, dec_recv)
        for j in range(group):
            dec_all[j] = jnp.broadcast_to(dec_rcv[j], (8, width))
        right = jnp.ones((8, width), F32)
        for j in range(group):
            right = right * dec_all[j]
            cum[j] = right
        left = jnp.ones((8, width), F32)
        for j in range(group - 1, -1, -1):
            left = left * dec_all[j]
            cum[j] = jnp.where(run == 1, cum[j], left)

    def part(b):
        return pl.ds(b * part_rows, part_rows)

    def third(b):
        return 3 * b // PARTS

    def relay_part(b):
        return relay.at[part(RELAYED.index(b))]

    def ship_copy(b, source):
        relayed = b in RELAYED
        return pltpu.make_async_remote_copy(
            src_ref=source.at[part(b)],
            dst_ref=relay_part(b) if relayed else stage.at[2, part(b)],
            send_sem=part_send,
            recv_sem=relay_recv.at[RELAYED.index(b)] if relayed else part_recv.at[third(b)],
            device_id=(relay_by if relayed else neighbour, cell),
            device_id_type=MESH,
        )

    def ship(*parts):
        for turn, other in enumerate((up_hbm, down_hbm)):

            @pl.when(jnp.logical_and(inner, way == turn))
            def _():
                for b in parts:
                    ship_copy(b, other).start()

    def hand_on(*parts):
        @pl.when(rank < 2)
        def _():
            for b in parts:
                all_of(relay_part(b), relay_recv.at[RELAYED.index(b)])
                pltpu.make_async_remote_copy(
                    src_ref=relay_part(b),
                    dst_ref=stage.at[2, part(b)],
                    send_sem=part_send,
                    recv_sem=part_recv.at[third(b)],
                    device_id=(across, cell),
                    device_id_type=MESH,
                ).start()

    def right_sweep(turn):
        right = jnp.zeros((8, width), F32)
        for j in range(group):
            right = dec_all[j] * right + fwd_rcv[turn, j]
            bwd_src[turn, j] = right
        return right

    def left_sweep(turn):
        left = jnp.zeros((8, width), F32)
        for j in range(group - 1, -1, -1):
            left = dec_all[j] * left + fwd_rcv[turn, j]
            lefts[j] = left
        return left

    def own_sweep(turn, meanwhile):
        all_of(fwd_rcv.at[turn], fwd_recv.at[turn])
        @pl.when(run == 0)
        def _():
            car_src[turn] = right_sweep(turn)

        @pl.when(run == 1)
        def _():
            car_src[turn] = left_sweep(turn)

        carry_copy(turn).start()

        @pl.when(run == 0)
        def _():
            left_sweep(turn)

        @pl.when(run == 1)
        def _():
            right_sweep(turn)

        meanwhile()
        carry_copy(turn).wait_recv()
        carry = car_rcv[turn]
        for j in range(group):
            bwd_src[turn, j] = bwd_src[turn, j] + lefts[j] + cum[j] * carry
        for offset in far_first(group):
            backward_copy(turn, peer(offset)).start()
        backward_own(turn).start()

    def chunk_rows(index):
        return pl.ds(index * chunk, chunk)

    def collected(turn, index):
        rows = chunk_rows(index)
        all_of(bwd_rcv.at[turn, rows], bwd_recv.at[turn, index])
        return anchor[rows, :] + lateral_weight * bwd_rcv[turn, rows, :]

    def prepare_main():
        @pl.when(rank > 0)
        def _():
            operator_load(down_hbm, 1).wait()
            for b in range(3):
                prepare(1, b, dep_high.at[0], dep_low.at[0])

    def prepare_other(b):
        all_of(stage.at[2, pl.ds(b * block, block)], part_recv.at[b])
        prepare(2, b, dep_high.at[1], dep_low.at[1])

    def first_meanwhile():
        ship(2, 3, 4, 7)

        @pl.when(rank == 1)
        def _():
            operator_load(down_hbm, 2).wait()
            for b in range(3):
                prepare(2, b, dep_high.at[1], dep_low.at[1])

    def second_meanwhile():
        ship(8, 9)
        hand_on(6)

        @pl.when(inner)
        def _():
            prepare_other(0)

    ship(1, 0)
    prepare_main()
    damping()
    own_sweep(0, first_meanwhile)
    ship(5, 6)
    hand_on(1)
    for index in range(CHUNKS):
        rows = chunk_rows(index)
        fwd_src[1, rows, :] = product(collected(0, index), lat_high[...], lat_low[...])
        send_forward(1, index)
    ship(10)
    hand_on(5)
    own_sweep(1, second_meanwhile)
    ship(11)
    hand_on(10)

    @pl.when(inner)
    def _():
        prepare_other(1)

    def depth_chunk(k):
        return pl.ds(pl.multiple_of(k * depth_rows, 8), depth_rows)

    def depth_copy(source, k, send, slot, target):
        rows = depth_chunk(k)
        return pltpu.make_async_remote_copy(
            src_ref=source.at[rows],
            dst_ref=dep_rcv.at[slot, rows],
            send_sem=dep_send.at[send],
            recv_sem=dep_recv.at[slot, k],
            device_id=(target, cell),
            device_id_type=MESH,
        )

    def arrived(slot, k):
        ref = dep_rcv.at[slot, depth_chunk(k)]
        pltpu.make_async_copy(ref, ref, dep_recv.at[slot, k]).wait()

    def mate_copy(index):
        rows = chunk_rows(index)
        return pltpu.make_async_remote_copy(
            src_ref=smooth.at[rows],
            dst_ref=mate.at[rows],
            send_sem=mate_send,
            recv_sem=mate_recv.at[index],
            device_id=(neighbour, cell),
            device_id_type=MESH,
        )

    for index in range(CHUNKS):
        rows = chunk_rows(index)
        smooth[rows, :] = collected(1, index)

        @pl.when(rank == 0)
        def _():
            for k in range(index * per_chunk, (index + 1) * per_chunk):
                depth_copy(smooth, k, 0, 0, chain_to).start()

        @pl.when(inner)
        def _():
            mate_copy(index).start()

    hand_on(11)

    def applied(c, which):
        return product(c, dep_high[which], dep_low[which])

    @pl.when(rank == 1)
    def _():
        @pl.loop(0, DEPTH_CHUNKS)
        def _(k):
            rows = depth_chunk(k)
            arrived(0, k)
            dep_src[0, rows, :] = smooth[rows, :] + applied(dep_rcv[0, rows, :], 0)
            depth_copy(dep_src.at[0], k, 0, 0, chain_to).start()
            out_ref[rows, :] = smooth[rows, :] + depth_weight * dep_rcv[0, rows, :]

        @pl.loop(0, DEPTH_CHUNKS)
        def _(k):
            rows = depth_chunk(k)
            arrived(1, k)
            dep_src[1, rows, :] = smooth[rows, :] + applied(dep_rcv[1, rows, :], 1)
            depth_copy(dep_src.at[1], k, 1, 1, back_to).start()
            out_ref[rows, :] = out_ref[rows, :] + depth_weight * dep_rcv[1, rows, :]

    @pl.when(rank == 0)
    def _():
        @pl.loop(0, DEPTH_CHUNKS)
        def _(k):
            rows = depth_chunk(k)
            arrived(1, k)
            out_ref[rows, :] = smooth[rows, :] + depth_weight * dep_rcv[1, rows, :]

    @pl.when(inner)
    def _():
        prepare_other(2)
        @pl.loop(0, DEPTH_CHUNKS)
        def _(k):
            rows = depth_chunk(k)
            arrived(0, k)
            near = smooth[rows, :] + applied(dep_rcv[0, rows, :], 0)
            dep_src[0, rows, :] = near
            for index in range(CHUNKS):

                @pl.when(k == index * per_chunk)
                def _():
                    all_of(mate.at[chunk_rows(index)], mate_recv.at[index])

            dep_src[1, rows, :] = mate[rows, :] + applied(near, 1)
            depth_copy(dep_src.at[1], k, 0, chain_slot, chain_to).start()
            depth_copy(dep_src.at[0], k, 1, 1, neighbour).start()
            out_ref[rows, :] = smooth[rows, :] + depth_weight * dep_rcv[0, rows, :]

        @pl.loop(0, DEPTH_CHUNKS)
        def _(k):
            rows = depth_chunk(k)
            arrived(1, k)
            out_ref[rows, :] = out_ref[rows, :] + depth_weight * dep_rcv[1, rows, :]

    peers = pl.ds(0, group - 1)
    for turn in range(PASSES):
        all_of(fwd_rcv.at[turn, peers], fwd_send.at[turn])
        all_of(bwd_src.at[turn, peers], bwd_send.at[turn])
        all_of(car_src.at[turn], car_send.at[turn])
    all_of(dec_rcv.at[peers], dec_send)
    all_of(smooth, dep_send.at[0])

    @pl.when(rank > 0)
    def _():
        all_of(smooth, dep_send.at[1])

    @pl.when(inner)
    def _():
        all_of(smooth, mate_send)
        all_of(stage.at[0], part_send)

    @pl.when(rank < 2)
    def _():
        all_of(relay, part_send)


def shards(source, rate, lat_op, down_op, up_op):
    order, columns = source.shape[2:]
    layers = lax.axis_size("depth")
    cells = lax.axis_size("lat")
    group = cells // 2
    width = order // 2
    any_space = pl.BlockSpec(memory_space=pl.ANY)
    vmem = pltpu.VMEM
    dma = pltpu.SemaphoreType.DMA
    traces = pl.pallas_call(
        functools.partial(kernel, layers, cells),
        name="sweeps",
        out_shape=jax.ShapeDtypeStruct((columns, order), F32),
        in_specs=[any_space] * 5,
        out_specs=pl.BlockSpec(memory_space=pltpu.VMEM),
        scratch_shapes=[
            vmem((columns, order), F32),
            vmem((1, order), F32),
            vmem((1, order), F32),
            vmem((3, order, order), F32),
            vmem((order, order), BF16),
            vmem((order, order), BF16),
            vmem((2, order, order), BF16),
            vmem((2, order, order), BF16),
            vmem((PASSES, columns, order), F32),
            vmem((PASSES, group, 8, width), F32),
            vmem((PASSES, 8, width), F32),
            vmem((PASSES, 8, width), F32),
            vmem((PASSES, group, 8, width), F32),
            vmem((PASSES, columns, order), F32),
            vmem((group, 1, width), F32),
            vmem((group, 8, width), F32),
            vmem((group, 8, width), F32),
            vmem((group, 8, width), F32),
            vmem((columns, order), F32),
            vmem((2, columns, order), F32),
            vmem((2, columns, order), F32),
            vmem((columns, order), F32),
            vmem((len(RELAYED) * (order // PARTS), order), F32),
            dma((7,)),
            dma,
            dma,
            dma((PASSES,)),
            dma((PASSES,)),
            dma((PASSES,)),
            dma((PASSES,)),
            dma((PASSES,)),
            dma((PASSES, CHUNKS)),
            dma((2,)),
            dma((2, DEPTH_CHUNKS)),
            dma,
            dma((CHUNKS,)),
            dma,
            dma((3,)),
            dma((len(RELAYED),)),
        ],
        compiler_params=pltpu.CompilerParams(
            collective_id=0, has_side_effects=True, vmem_limit_bytes=56200000
        ),
    )(
        source.reshape(order, columns).T,
        rate.reshape(1, order),
        lat_op.reshape(order, order),
        down_op.reshape(order, order),
        up_op.reshape(order, order),
    )
    return traces.T.reshape(1, 1, order, columns)


def solution(mesh):
    spec = P("depth", "lat", None, None)
    in_specs = (spec, P("depth", "lat", None), spec, spec, spec)
    return jax.shard_map(shards, mesh=mesh, in_specs=in_specs, out_specs=spec, check_vma=False)
```
